256 devices in a mesh: band: 8 (over y, core), plane: 32 (over x, z).
Axes of the slice: x: 4, y: 4, z: 8, core: 2. Of those that a mesh axis runs over, the one named last changes fastest.
Arguments:
- psi: float32 [2, 8, 4096, 128], P(None, 'band', 'plane'), may hold values from -8 to 8
- potential: float32 [96, 9216], P('plane'), may hold values from 0 to 2
- stick_column: int32 [4096], P('plane'), may hold values from 0 to 9215, as said below
- stick_length: int32 [4096], P('plane'), may hold values from 0 to 49, as said below
Outputs:
- psi_new: float32 [2, 8, 4096, 128], P(None, 'band', 'plane')
- potential_new: float32 [96, 9216], P('plane')
The draws below stay inside these ranges and needn't reach their ends.
Inputs may be any that keep to these rules, and one draw needn't show every extreme that they name: `stick_column`: within each device's block of 128 slots the live sticks come first and the other slots are empty with column 0. Over all devices the live slots hold every column (mx mod 96) * 96 + (my mod 96) with mx * mx + my * my <= 576 exactly once, in an order drawn from the seed; some device's block is full and the others hold fewer. `stick_length`: A live slot's length is 2 h + 1, with h the largest whole number such that mx * mx + my * my + h * h <= 576 for its column; empty slots have length 0.
All inputs are finite; a program needn't handle non-finite values.
Results may differ from the reference program's by a relative error of at most 0.0001.
Values sent between devices are 32-bit elements; how exact they have to be, the bound alone decides.
No kernel may reach another device: no remote copies, remote signals or barrier semaphores. Data moves between devices by JAX's collectives and lax.ppermute only.
A program may use at most 64 MiB of HBM per device.

```python
import math
import jax
import jax.numpy as jnp
import numpy as np
from jax import lax

NG = 96
RAD = 24
STICK_COEFFS = 128
BAND_DEV = 1
BAND_TOTAL = 8
SLOTS_PER_DEVICE = 128
SLOT_TOTAL = 4096
NXY = 9216


def disc_table():
    rows = np.arange(-RAD, RAD + 1)
    first, second = np.meshgrid(rows, rows, indexing='ij')
    first = first.reshape(-1)
    second = second.reshape(-1)
    room = RAD * RAD - first * first - second * second
    keep = room >= 0
    first = first[keep]
    second = second[keep]
    room = room[keep]
    height = np.array([math.isqrt(int(value)) for value in room], dtype=np.int64)
    columns = first % NG * NG + second % NG
    return (columns.astype(np.int32), (2 * height + 1).astype(np.int32))


def stick_layout(key):
    columns, lengths = disc_table()
    count = columns.shape[0]
    device_list = SLOT_TOTAL // SLOTS_PER_DEVICE
    order_key, full_key, weight_key = jax.random.split(jax.random.fold_in(key, 7), 3)
    order = jax.random.permutation(order_key, count)
    fullest = jax.random.randint(full_key, (), 0, device_list)
    device_ids = jnp.arange(device_list, dtype=jnp.int32)
    weights = jax.random.randint(weight_key, (device_list,), 2, 4)
    weights = jnp.where(device_ids == fullest, 0, weights)
    remaining = count - SLOTS_PER_DEVICE
    shares = remaining * weights // jnp.sum(weights)
    shares = jnp.minimum(shares, SLOTS_PER_DEVICE)
    shares = jnp.where(device_ids == fullest, SLOTS_PER_DEVICE, shares)
    leftover = count - jnp.sum(shares)
    spaces = SLOTS_PER_DEVICE - shares
    before = jnp.cumsum(spaces) - spaces
    shares = shares + jnp.clip(leftover - before, 0, spaces)
    starts = jnp.cumsum(shares) - shares
    slot_numbers = jnp.arange(SLOT_TOTAL, dtype=jnp.int32)
    holder = slot_numbers // SLOTS_PER_DEVICE
    within = slot_numbers % SLOTS_PER_DEVICE
    live = within < shares[holder]
    chosen = jnp.clip(starts[holder] + within, 0, count - 1)
    stick = order[chosen]
    column_ids = jnp.where(live, jnp.asarray(columns)[stick], 0).astype(jnp.int32)
    length_ids = jnp.where(live, jnp.asarray(lengths)[stick], 0).astype(jnp.int32)
    return (column_ids, length_ids)


def draw_stick_column(key, part):
    return stick_layout(key)[0]


def draw_stick_length(key, part):
    return stick_layout(key)[1]


def block_levels(own_key, dims, cuts, smallest, top_value):
    def one(position, blocks):
        draws = jax.random.uniform(jax.random.fold_in(jax.random.fold_in(own_key, 6), position), (blocks,), jnp.float32, smallest / len(cuts), top_value / len(cuts))
        return jnp.repeat(jnp.exp(draws), dims[position] // blocks).reshape((-1,) + (1,) * (len(dims) - position - 1))

    level = one(*cuts[0])
    for cut in cuts[1:]:
        level = level * one(*cut)
    return level


def gaussian(key, dims, spread, most, shards=(), kind=jnp.bfloat16):
    entries = jax.random.normal(key, dims, jnp.float32) * spread
    if len(shards) > 0:
        entries = block_levels(key, dims, shards, -0.22, 0.18) * entries
    return jnp.clip(entries, min=-most, max=most).astype(kind)


def setup_inputs(seed: int = 0) -> dict:
    seeds = jax.random.split(jax.random.key(seed), 5)
    psi = gaussian(seeds[0], (2, BAND_TOTAL, SLOT_TOTAL, STICK_COEFFS), 2.0, 8.0, ((1, 8), (2, 32)), jnp.float32)
    potential = jnp.clip(2.0 * jax.random.uniform(seeds[1], (NG, NXY), jnp.float32) ** block_levels(seeds[1], (NG, NXY), ((0, 32),), -0.2, 0.2), 0.0, 2.0)
    stick_column = draw_stick_column(jax.random.fold_in(seeds[4], 71), 0)
    stick_length = draw_stick_length(jax.random.fold_in(seeds[4], 71), 0)
    return {"psi": psi, "potential": potential, "stick_column": stick_column, "stick_length": stick_length}


TIMESTEP = 0.6
LINEAR_GAIN = 0.5
CUBIC_GAIN = 0.3


def reference(psi, potential, stick_column, stick_length):
    order = jnp.arange(STICK_COEFFS, dtype=jnp.int32)
    half = (stick_length - 1) // 2
    mask = (order[None, :] < stick_length[:, None]).astype(jnp.float32)
    first = stick_column // NG
    second = stick_column % NG
    signed_first = jnp.where(first > NG // 2, first - NG, first)
    signed_second = jnp.where(second > NG // 2, second - NG, second)
    depth = order[None, :] - half[:, None]
    kinetic = ((signed_first * signed_first + signed_second * signed_second)[:, None] + depth * depth).astype(jnp.float32) / (RAD * RAD) * mask
    wrapped = (depth % NG).astype(jnp.int32)
    leading_index = first[:, None].astype(jnp.int32)
    second_index = second[:, None].astype(jnp.int32)
    field_potential = potential.reshape(NG, NG, NG).transpose(1, 2, 0)
    norm = float(NG) ** 1.5

    def synthesis(coefficients):
        grid = jnp.zeros((NG, NG, NG), coefficients.dtype).at[leading_index, second_index, wrapped].add(coefficients)
        return jnp.fft.ifftn(grid) * norm

    def analysis(values):
        spectrum = jnp.fft.fftn(values) / norm
        return spectrum[leading_index, second_index, wrapped] * mask

    def hamiltonian(coefficients):
        return kinetic * coefficients + analysis(field_potential * synthesis(coefficients))

    def one_band(carry, pair):
        term = lax.complex(pair[0], pair[1]) * mask
        start = synthesis(term)
        total = term
        for power in range(1, 4):
            term = (-1j * (TIMESTEP / power)) * hamiltonian(term)
            total = total + term
        final = synthesis(total)
        change = jnp.real(final) ** 2 + jnp.imag(final) ** 2 - jnp.real(start) ** 2 - jnp.imag(start) ** 2
        return carry + change, jnp.stack([jnp.real(total), jnp.imag(total)])

    bands_first = jnp.moveaxis(psi, 1, 0)
    summed, coefficients = lax.scan(one_band, jnp.zeros((NG, NG, NG), jnp.float32), bands_first)
    psi_new = jnp.moveaxis(coefficients, 0, 1)
    delta = (summed / BAND_DEV).transpose(2, 0, 1).reshape(NG, NG * NG)
    potential_new = potential + LINEAR_GAIN * delta + CUBIC_GAIN * delta * delta * delta
    return psi_new, potential_new
```

```python
import functools
import math

import jax
import jax.numpy as jnp
import ml_dtypes
import numpy as np
from jax import lax
from jax.experimental import pallas as pl
from jax.experimental.pallas import tpu as pltpu
from jax.sharding import Mesh
from jax.sharding import PartitionSpec as P

NG = 96
RAD = 24
HALF = 64
LANES = 128
PLANES = 3
OWNERS = 32
SLOTS = 128
TIMESTEP = 0.6
LINEAR_GAIN = 0.5
CUBIC_GAIN = 0.3

F32 = jnp.float32
BF16 = jnp.bfloat16
NT = (((1,), (1,)), ((), ()))


def halves(values):
    high = values.astype(ml_dtypes.bfloat16)
    low = (values - high.astype(np.float64)).astype(ml_dtypes.bfloat16)
    return high, low


def wave(count, order):
    turns = np.outer(np.arange(count), np.arange(order) - RAD) % NG
    angle = turns * (2.0 * math.pi / NG)
    scale = NG**-0.5
    return np.cos(angle) * scale, np.sin(angle) * scale


def height_table():
    cosine, sine = wave(NG, 2 * RAD + 1)
    table = np.zeros((OWNERS, 8, LANES))
    order = 2 * RAD + 1
    for owner in range(OWNERS):
        for plane in range(PLANES):
            z = PLANES * owner + plane
            table[owner, 2 * plane, :order] = cosine[z]
            table[owner, 2 * plane, HALF : HALF + order] = -sine[z]
            table[owner, 2 * plane + 1, :order] = sine[z]
            table[owner, 2 * plane + 1, HALF : HALF + order] = cosine[z]
    return table.reshape(OWNERS * 8, LANES)


def second_table():
    cosine, sine = wave(NG, 2 * RAD + 1)
    order = 2 * RAD + 1
    table = np.zeros((LANES, 2 * LANES))
    table[:order, :NG] = cosine.T
    table[HALF : HALF + order, :NG] = -sine.T
    table[:order, LANES : LANES + NG] = sine.T
    table[HALF : HALF + order, LANES : LANES + NG] = cosine.T
    return table


def first_table():
    cosine, sine = wave(NG, 2 * RAD + 1)
    table = np.zeros((2 * NG, HALF))
    table[:NG, : 2 * RAD + 1] = cosine
    table[NG:, : 2 * RAD + 1] = sine
    return table


def tables():
    high, low = halves(height_table())
    second_high, second_low = halves(second_table())
    first_high, first_low = halves(first_table())
    back = np.concatenate([first_table()[:NG].T, first_table()[NG:].T], axis=0)
    back_high, back_low = halves(back)
    stick = (
        np.concatenate([high, high], axis=1),
        low,
        high,
    )
    plane = (
        np.concatenate([second_high, second_high], axis=0),
        second_low,
        np.concatenate([first_high, first_low, first_high], axis=1),
        np.concatenate([back_high, back_low, back_high], axis=1),
        np.ascontiguousarray(second_high.T),
        np.ascontiguousarray(second_low.T),
    )
    return stick, plane


def split(values):
    high = values.astype(BF16)
    return high, (values - high.astype(F32)).astype(BF16)


def dot(left, right):
    return jnp.dot(left, right, preferred_element_type=F32)


def lanes_of(shape):
    return lax.broadcasted_iota(jnp.int32, shape, 1)


def stick_codes(column, length):
    first = jnp.floor((column + 0.5) * (1.0 / NG))
    second = column - NG * first
    first = jnp.where(first > NG // 2, first - NG, first)
    second = jnp.where(second > NG // 2, second - NG, second)
    live = length > 0.0
    return jnp.where(live, first + RAD, -1.0), jnp.where(live, second + RAD, -1.0)


def along_slots(row):
    return jnp.broadcast_to(row, (SLOTS, LANES)).T


def shift_lanes(values, amount, direction):
    for bit in range(5):
        step = 1 << bit
        moved = pltpu.roll(values, step if direction > 0 else LANES - step, 1)
        values = jnp.where((amount & step) != 0, moved, values)
    return values


def lane_shift(length_row):
    length = along_slots(length_row).astype(jnp.int32)
    return jnp.clip(RAD - ((length - 1) >> 1), 0, RAD), length


def send_heights(term, codes, stick_pair, stick_low, out_ref):
    high, low = split(term)
    both = jnp.concatenate([high, low], axis=1)
    rows = lax.dot_general(stick_pair, both, NT, preferred_element_type=F32)
    rows = rows + lax.dot_general(stick_low, high, NT, preferred_element_type=F32)
    rows = rows.reshape(OWNERS, 8, SLOTS)
    place = lax.broadcasted_iota(jnp.int32, (OWNERS, 8, SLOTS), 1)
    rows = jnp.where(place == 6, codes[0][None], rows)
    out_ref[...] = jnp.where(place == 7, codes[1][None], rows)


def start_kernel(psi_ref, column_ref, length_ref, pair_ref, low_ref, term_ref, kinetic_ref, out_ref):
    column, length_row = column_ref[...], length_ref[...]
    codes = stick_codes(column, length_row)
    amount, length = lane_shift(length_row)
    lane = lanes_of((SLOTS, LANES))
    inside = lane < length
    real_part = shift_lanes(jnp.where(inside, psi_ref[0], 0.0), amount, 1)
    imag_part = shift_lanes(jnp.where(inside, psi_ref[1], 0.0), amount, 1)
    term = real_part + pltpu.roll(imag_part, HALF, 1)
    term_ref[...] = term
    depth = (lane & (HALF - 1)) - RAD
    first = along_slots(codes[0]) - RAD
    second = along_slots(codes[1]) - RAD
    spread = depth.astype(F32)
    kinetic = (first * first + second * second + spread * spread) / (RAD * RAD)
    valid = (jnp.abs(depth) <= ((length - 1) >> 1)) & (length > 0)
    kinetic_ref[...] = jnp.where(valid, kinetic, -1.0)
    send_heights(term, codes, pair_ref[...], low_ref[...], out_ref)


def stick_kernel(power, last, *refs):
    if last:
        (got_ref, term_ref, total_ref, kinetic_ref, column_ref, length_ref, pair_ref, low_ref, high_ref,
         psi_ref, out_ref) = refs
    else:
        (got_ref, term_ref, total_ref, kinetic_ref, column_ref, length_ref, pair_ref, low_ref, high_ref,
         next_ref, sum_ref, out_ref) = refs
    codes = stick_codes(column_ref[...], length_ref[...])
    got = got_ref[...].reshape(OWNERS * 8, SLOTS).T
    high, low = split(got)
    back_high, back_low = high_ref[...], low_ref[...]
    applied = dot(high, back_high) + dot(low, back_high) + dot(high, back_low)
    kinetic = kinetic_ref[...]
    applied = jnp.where(kinetic >= 0.0, applied + kinetic * term_ref[...], 0.0)
    factor = TIMESTEP / power
    lane = lanes_of((SLOTS, LANES))
    term = pltpu.roll(applied, HALF, 1) * jnp.where(lane < HALF, factor, -factor)
    total = total_ref[...] + term
    if last:
        amount, _ = lane_shift(length_ref[...])
        lower = lane < HALF
        psi_ref[0] = shift_lanes(jnp.where(lower, total, 0.0), amount, -1)
        psi_ref[1] = shift_lanes(jnp.where(lower, pltpu.roll(total, HALF, 1), 0.0), amount, -1)
        send_heights(total, codes, pair_ref[...], low_ref[...], out_ref)
    else:
        next_ref[...] = term
        sum_ref[...] = total
        send_heights(term, codes, pair_ref[...], low_ref[...], out_ref)


def plane_kernel(stage, *refs):
    refs = list(refs)
    got_ref = refs.pop(0)
    other_ref = refs.pop(0)
    second_pair, second_low, first_all, back_all, inner_high, inner_low = refs[:6]
    refs = refs[6:]
    spread_ref, cell_ref = refs[-2:]
    outs = refs[:-2]
    row = lax.broadcasted_iota(jnp.int32, (HALF, SLOTS), 0).astype(F32)

    def place(owner, carry):
        got = got_ref[owner]
        high = got.astype(BF16).astype(F32)
        low = got - high
        at = pl.ds(pl.multiple_of(owner * SLOTS, SLOTS), SLOTS)
        mine = row == got[6:7]
        for r in range(2 * PLANES):
            spread_ref[r * HALF : (r + 1) * HALF, at] = jnp.where(mine, high[r : r + 1], 0.0).astype(BF16)
            spread_ref[(r + 6) * HALF : (r + 7) * HALF, at] = jnp.where(mine, low[r : r + 1], 0.0).astype(BF16)
        cell = jnp.where(row == got[7:8], 1.0, 0.0).astype(BF16)
        cell_ref[:HALF, at] = cell
        cell_ref[HALF:, at] = cell
        return carry

    lax.fori_loop(0, OWNERS, place, 0, unroll=4)
    grid = lax.dot_general(spread_ref[...], cell_ref[:HALF], NT, preferred_element_type=F32)
    grid = (grid[: 6 * HALF] + grid[6 * HALF :]).reshape(PLANES, 2, HALF, HALF)
    lined = jnp.concatenate([grid[:, 0], grid[:, 1]], axis=2).reshape(PLANES * HALF, LANES)
    high, low = split(lined)
    middle = dot(jnp.concatenate([high, low], axis=1), second_pair[...]) + dot(high, second_low[...])
    returned = []
    for plane in range(PLANES):
        high, low = split(middle[plane * HALF : (plane + 1) * HALF])
        both = dot(first_all[...], jnp.concatenate([high, high, low], axis=0))
        real_part = both[:NG, :LANES] - both[NG:, LANES:]
        imag_part = both[NG:, :LANES] + both[:NG, LANES:]
        if stage == "first":
            outs[1][plane] = real_part * real_part + imag_part * imag_part
        if stage == "last":
            outs[0][plane] = real_part * real_part + imag_part * imag_part - other_ref[plane]
            continue
        weight = other_ref[plane]
        field = jnp.concatenate([real_part * weight, imag_part * weight], axis=1)
        high, low = split(field)
        both = dot(back_all[...], jnp.concatenate([high, high, low], axis=0))
        returned.append(
            jnp.concatenate(
                [both[:HALF, :LANES] + both[HALF:, LANES:], both[:HALF, LANES:] - both[HALF:, :LANES]],
                axis=1,
            )
        )
    if stage == "last":
        return
    high, low = split(jnp.concatenate(returned, axis=0))
    rows = dot(high, inner_high[...]) + dot(low, inner_high[...]) + dot(high, inner_low[...])
    rows = rows.reshape(PLANES, 1, HALF, LANES)
    rows = jnp.concatenate([rows[..., :HALF], rows[..., HALF:]], axis=1).reshape(6 * HALF, HALF)
    high, low = split(rows)
    both = jnp.concatenate([high, low], axis=1)
    tail = jnp.zeros((2, SLOTS), F32)

    def pick(pair, carry):
        at = pl.ds(pl.multiple_of(pair * 2 * SLOTS, 2 * SLOTS), 2 * SLOTS)
        found = dot(both, cell_ref[:, at]).reshape(6, HALF, 2 * SLOTS)
        for side in range(2):
            mine = row == got_ref[2 * pair + side][6:7]
            chosen = jnp.where(mine[None], found[:, :, side * SLOTS : (side + 1) * SLOTS], 0.0)
            outs[0][2 * pair + side] = jnp.concatenate([jnp.sum(chosen, axis=1), tail], axis=0)
        return carry

    lax.fori_loop(0, OWNERS // 2, pick, 0, unroll=4)


def call(kernel, name, shapes, scratch=()):
    return pl.pallas_call(
        kernel,
        out_shape=tuple(jax.ShapeDtypeStruct(s, F32) for s in shapes),
        scratch_shapes=scratch,
        name=name,
        compiler_params=pltpu.CompilerParams(vmem_limit_bytes=48 << 20),
    )


def plane_call(stage, got, other, plane_tables):
    wire = (OWNERS, 8, SLOTS)
    cells = (PLANES, NG, LANES)
    shapes = {"first": (wire, cells), "next": (wire,), "last": (cells,)}[stage]
    scratch = [pltpu.VMEM((12 * HALF, OWNERS * SLOTS), BF16), pltpu.VMEM((2 * HALF, OWNERS * SLOTS), BF16)]
    return call(functools.partial(plane_kernel, stage), "plane_" + stage, shapes, scratch)(got, other, *plane_tables)


def exchange(rows):
    return lax.all_to_all(rows, ("x", "z"), split_axis=0, concat_axis=0, tiled=True)


def swap(values, axis, mask):
    size = lax.axis_size(axis)
    return lax.ppermute(values, axis, [(s, s ^ mask) for s in range(size)])


def shards(psi, potential, stick_column, stick_length):
    stick_np, plane_np = tables()
    stick_tables = tuple(map(jnp.asarray, stick_np))
    plane_tables = tuple(map(jnp.asarray, plane_np))
    wire, state = (OWNERS, 8, SLOTS), (SLOTS, LANES)
    column = stick_column.astype(F32).reshape(1, SLOTS)
    length = stick_length.astype(F32).reshape(1, SLOTS)
    weight = jnp.pad(potential.reshape(PLANES, NG, NG), ((0, 0), (0, 0), (0, LANES - NG)))
    term, kinetic, rows = call(start_kernel, "start", (state, state, wire))(
        psi.reshape(2, SLOTS, LANES), column, length, *stick_tables[:2]
    )
    total = term
    before = None
    psi_new = None
    for power in range(1, 4):
        got = exchange(rows)
        if power == 1:
            rows, before = plane_call("first", got, weight, plane_tables)
        else:
            (rows,) = plane_call("next", got, weight, plane_tables)
        got = exchange(rows)
        last = power == 3
        shapes = ((2, SLOTS, LANES), wire) if last else (state, state, wire)
        given = call(functools.partial(stick_kernel, power, last), f"stick_{power}", shapes)(
            got, term, total, kinetic, column, length, *stick_tables
        )
        if last:
            psi_new, rows = given
        else:
            term, total, rows = given
    (change,) = plane_call("last", exchange(rows), before, plane_tables)
    change = change + swap(change, "core", 1)
    change = change + swap(change, "y", 1)
    change = change + swap(change, "y", 2)
    added = weight + LINEAR_GAIN * change + CUBIC_GAIN * change * change * change
    potential_new = added[:, :, :NG].reshape(PLANES, NG * NG)
    return psi_new.reshape(2, 1, SLOTS, LANES), potential_new


def solution(mesh):
    fine = Mesh(mesh.devices.reshape(4, 2, 4, 8), ("y", "core", "x", "z"))
    band, plane = ("y", "core"), ("x", "z")
    in_specs = (P(None, band, plane, None), P(plane, None), P(plane), P(plane))
    out_specs = (P(None, band, plane, None), P(plane, None))
    return jax.shard_map(shards, mesh=fine, in_specs=in_specs, out_specs=out_specs, check_vma=False)
```

```python
import functools
import math

import jax
import jax.numpy as jnp
import ml_dtypes
import numpy as np
from jax import lax
from jax.experimental import pallas as pl
from jax.experimental.pallas import tpu as pltpu
from jax.sharding import Mesh
from jax.sharding import PartitionSpec as P

NG = 96
RAD = 24
HALF = 64
LANES = 128
PLANES = 3
OWNERS = 32
SLOTS = 128
ROWS = 16
CHUNK = 4
CELLS = CHUNK * HALF
SHARE = PLANES * NG // 2
PARTS = 2 * PLANES
TIMESTEP = 0.6
LINEAR_GAIN = 0.5
CUBIC_GAIN = 0.3

F32 = jnp.float32
BF16 = jnp.bfloat16
NT = (((1,), (1,)), ((), ()))


def halves(values):
    high = values.astype(ml_dtypes.bfloat16)
    low = (values - high.astype(np.float64)).astype(ml_dtypes.bfloat16)
    return high, low


def wave(count, order):
    turns = np.outer(np.arange(count), np.arange(order) - RAD) % NG
    angle = turns * (2.0 * math.pi / NG)
    scale = NG**-0.5
    return np.cos(angle) * scale, np.sin(angle) * scale


def height_table():
    cosine, sine = wave(NG, 2 * RAD + 1)
    table = np.zeros((OWNERS, 8, LANES))
    order = 2 * RAD + 1
    for owner in range(OWNERS):
        for plane in range(PLANES):
            z = PLANES * owner + plane
            table[owner, 2 * plane, :order] = cosine[z]
            table[owner, 2 * plane, HALF : HALF + order] = -sine[z]
            table[owner, 2 * plane + 1, :order] = sine[z]
            table[owner, 2 * plane + 1, HALF : HALF + order] = cosine[z]
    return table.reshape(OWNERS * 8, LANES)


def second_table():
    cosine, sine = wave(NG, 2 * RAD + 1)
    order = 2 * RAD + 1
    table = np.zeros((LANES, 2 * LANES))
    table[:order, :NG] = cosine.T
    table[HALF : HALF + order, :NG] = -sine.T
    table[:order, LANES : LANES + NG] = sine.T
    table[HALF : HALF + order, LANES : LANES + NG] = cosine.T
    return table


def first_table():
    cosine, sine = wave(NG, 2 * RAD + 1)
    table = np.zeros((2 * NG, HALF))
    table[:NG, : 2 * RAD + 1] = cosine
    table[NG:, : 2 * RAD + 1] = sine
    return table


def tables():
    high, low = halves(height_table())
    order = np.arange(HALF)
    order = CHUNK * (order % ROWS) + order // ROWS
    second_high, second_low = halves(second_table())
    first = first_table()[:, order]
    first_high, first_low = halves(first)
    back = np.concatenate([first[:NG].T, first[NG:].T], axis=0)
    back_high, back_low = halves(back)
    stick = np.concatenate([high, low], axis=1)
    plane = (
        np.concatenate([second_high, second_high], axis=0),
        second_low,
        np.concatenate([first_high, first_low, first_high], axis=1),
        np.concatenate([back_high, back_low, back_high], axis=1),
        np.ascontiguousarray(second_high.T),
        np.ascontiguousarray(second_low.T),
    )
    return stick, plane


def split(values):
    high = values.astype(BF16)
    return high, (values - high.astype(F32)).astype(BF16)


def dot(left, right):
    return jnp.dot(left, right, preferred_element_type=F32)


def lanes_of(shape):
    return lax.broadcasted_iota(jnp.int32, shape, 1)


def signed_indices(column):
    first = jnp.floor((column + 0.5) * (1.0 / NG))
    second = column - NG * first
    first = jnp.where(first > NG // 2, first - NG, first)
    second = jnp.where(second > NG // 2, second - NG, second)
    return first + RAD, second + RAD


def cell_codes(first, second, length):
    row = jnp.floor((first + 0.5) * (1.0 / CHUNK))
    place = (first - CHUNK * row) * HALF + second
    live = length > 0.0
    return jnp.where(live, row, -1.0), jnp.where(live, place, -1.0)


def along_slots(row):
    return jnp.broadcast_to(row, (SLOTS, LANES)).T


def shift_lanes(values, amount, direction):
    for bit in range(5):
        step = 1 << bit
        moved = pltpu.roll(values, step if direction > 0 else LANES - step, 1)
        values = jnp.where((amount & step) != 0, moved, values)
    return values


def lane_shift(length_row):
    length = along_slots(length_row).astype(jnp.int32)
    return jnp.clip(RAD - ((length - 1) >> 1), 0, RAD), length


def send_heights(term, codes, stick_ref, out_ref):
    high, low = split(term)
    both = jnp.concatenate([high, low], axis=1)
    table_high, table_low = stick_ref[:, :LANES], stick_ref[:, LANES:]
    pair = jnp.concatenate([table_high, table_high], axis=1)
    rows = lax.dot_general(pair, both, NT, preferred_element_type=F32)
    rows = rows + lax.dot_general(table_low, high, NT, preferred_element_type=F32)
    rows = rows.reshape(OWNERS, 8, SLOTS)
    place = lax.broadcasted_iota(jnp.int32, (OWNERS, 8, SLOTS), 1)
    rows = jnp.where(place == 6, codes[0][None], rows)
    out_ref[...] = jnp.where(place == 7, codes[1][None], rows)


def slot_rows(column_ref, length_ref):
    column = column_ref[...].astype(F32).reshape(1, SLOTS)
    return column, length_ref[...].astype(F32).reshape(1, SLOTS)


def start_kernel(psi_ref, column_ref, length_ref, stick_ref, term_ref, kinetic_ref, out_ref):
    column, length_row = slot_rows(column_ref, length_ref)
    first, second = signed_indices(column)
    codes = cell_codes(first, second, length_row)
    amount, length = lane_shift(length_row)
    lane = lanes_of((SLOTS, LANES))
    inside = lane < length
    real_part = shift_lanes(jnp.where(inside, psi_ref[0], 0.0), amount, 1)
    imag_part = shift_lanes(jnp.where(inside, psi_ref[1], 0.0), amount, 1)
    term = real_part + pltpu.roll(imag_part, HALF, 1)
    term_ref[...] = term
    depth = (lane & (HALF - 1)) - RAD
    spread = depth.astype(F32)
    first, second = first - RAD, second - RAD
    flat = along_slots(first * first + second * second)
    kinetic = (flat + spread * spread) / (RAD * RAD)
    valid = (jnp.abs(depth) <= ((length - 1) >> 1)) & (length > 0)
    kinetic_ref[...] = jnp.where(valid, kinetic, -1.0)
    send_heights(term, codes, stick_ref, out_ref)


def stick_kernel(power, last, *refs):
    got_ref, term_ref, total_ref, kinetic_ref, column_ref, length_ref, stick_ref = refs[:7]
    outs = refs[7:]
    out_ref = outs[-1]
    column, length_row = slot_rows(column_ref, length_ref)
    codes = cell_codes(*signed_indices(column), length_row)
    got = got_ref[...].reshape(OWNERS * 8, SLOTS).T
    high, low = split(got)
    back_high, back_low = stick_ref[:, :LANES], stick_ref[:, LANES:]
    applied = dot(high, back_high) + dot(low, back_high) + dot(high, back_low)
    kinetic = kinetic_ref[...]
    applied = jnp.where(kinetic >= 0.0, applied + kinetic * term_ref[...], 0.0)
    factor = TIMESTEP / power
    lane = lanes_of((SLOTS, LANES))
    term = pltpu.roll(applied, HALF, 1) * jnp.where(lane < HALF, factor, -factor)
    total = total_ref[...] + term
    if last:
        amount, _ = lane_shift(length_row)
        lower = lane < HALF
        psi_ref = outs[0]
        psi_ref[0] = shift_lanes(jnp.where(lower, total, 0.0), amount, -1)
        psi_ref[1] = shift_lanes(jnp.where(lower, pltpu.roll(total, HALF, 1), 0.0), amount, -1)
        send_heights(total, codes, stick_ref, out_ref)
    else:
        outs[0][...] = term
        outs[1][...] = total
        send_heights(term, codes, stick_ref, out_ref)


def plane_kernel(stage, *refs):
    refs = list(refs)
    got_ref = refs.pop(0)
    other_ref = refs.pop(0)
    core_ref = refs.pop(0) if stage == "last" else None
    second_pair, second_low, first_all, back_all, inner_high, inner_low = refs[:6]
    refs = refs[6:]
    spread_ref, cell_ref = refs[-2:]
    outs = refs[:-2]
    row = lax.broadcasted_iota(jnp.int32, (ROWS, SLOTS), 0).astype(F32)
    cell = lax.broadcasted_iota(jnp.int32, (CELLS, SLOTS), 0).astype(F32)

    def place(owner, carry):
        got = got_ref[owner]
        high = got.astype(BF16).astype(F32)
        low = got - high
        at = pl.ds(pl.multiple_of(owner * SLOTS, SLOTS), SLOTS)
        mine = row == got[6:7]
        for r in range(PARTS):
            here, there = r * ROWS, (r + PARTS) * ROWS
            spread_ref[here : here + ROWS, at] = jnp.where(mine, high[r : r + 1], 0.0).astype(BF16)
            spread_ref[there : there + ROWS, at] = jnp.where(mine, low[r : r + 1], 0.0).astype(BF16)
        cell_ref[:, at] = jnp.where(cell == got[7:8], 1.0, 0.0).astype(BF16)
        return carry

    lax.fori_loop(0, OWNERS, place, 0, unroll=4)
    grid = lax.dot_general(spread_ref[...], cell_ref[...], NT, preferred_element_type=F32)
    grid = (grid[: PARTS * ROWS] + grid[PARTS * ROWS :]).reshape(PLANES, 2, ROWS, CELLS)
    pieces = [
        jnp.concatenate([grid[:, part, :, c * HALF : (c + 1) * HALF] for part in range(2)], axis=2)
        for c in range(CHUNK)
    ]
    lined = jnp.stack(pieces, axis=1).reshape(PLANES * HALF, LANES)
    high, low = split(lined)
    middle = dot(jnp.concatenate([high, low], axis=1), second_pair[...]) + dot(high, second_low[...])
    returned = []
    for plane in range(PLANES):
        high, low = split(middle[plane * HALF : (plane + 1) * HALF])
        both = dot(first_all[...], jnp.concatenate([high, high, low], axis=0))
        real_part = both[:NG, :LANES] - both[NG:, LANES:]
        imag_part = both[NG:, :LANES] + both[:NG, LANES:]
        if stage == "first":
            outs[1][plane] = real_part * real_part + imag_part * imag_part
        if stage == "last":
            returned.append(real_part * real_part + imag_part * imag_part - other_ref[plane])
            continue
        weight = other_ref[plane]
        field = jnp.concatenate([real_part * weight, imag_part * weight], axis=1)
        high, low = split(field)
        both = dot(back_all[...], jnp.concatenate([high, high, low], axis=0))
        returned.append(
            jnp.concatenate(
                [both[:HALF, :LANES] + both[HALF:, LANES:], both[:HALF, LANES:] - both[HALF:, :LANES]],
                axis=1,
            )
        )
    if stage == "last":
        change = jnp.concatenate(returned, axis=0)
        upper, lower = change[:SHARE], change[SHARE:]
        mine = core_ref[0] == 0
        outs[0][...] = jnp.where(mine, upper, lower)
        outs[1][...] = jnp.where(mine, lower, upper)
        return
    high, low = split(jnp.concatenate(returned, axis=0))
    rows = dot(high, inner_high[...]) + dot(low, inner_high[...]) + dot(high, inner_low[...])
    rows = rows.reshape(PLANES, CHUNK, ROWS, LANES)
    pieces = [
        jnp.concatenate([rows[:, c, :, part * HALF : (part + 1) * HALF] for c in range(CHUNK)], axis=2)
        for part in range(2)
    ]
    high, low = split(jnp.stack(pieces, axis=1).reshape(PARTS * ROWS, CELLS))
    both = jnp.concatenate([high, low], axis=0)
    tail = jnp.zeros((2, SLOTS), F32)

    def pick(pair, carry):
        at = pl.ds(pl.multiple_of(pair * 2 * SLOTS, 2 * SLOTS), 2 * SLOTS)
        found = dot(both, cell_ref[:, at])
        found = (found[: PARTS * ROWS] + found[PARTS * ROWS :]).reshape(PARTS, ROWS, 2 * SLOTS)
        for side in range(2):
            mine = row == got_ref[2 * pair + side][6:7]
            chosen = jnp.where(mine[None], found[:, :, side * SLOTS : (side + 1) * SLOTS], 0.0)
            outs[0][2 * pair + side] = jnp.concatenate([jnp.sum(chosen, axis=1), tail], axis=0)
        return carry

    lax.fori_loop(0, OWNERS // 2, pick, 0, unroll=4)


def call(kernel, name, shapes, scratch=(), **more):
    return pl.pallas_call(
        kernel,
        out_shape=tuple(jax.ShapeDtypeStruct(s, F32) for s in shapes),
        scratch_shapes=scratch,
        name=name,
        compiler_params=pltpu.CompilerParams(vmem_limit_bytes=48 << 20),
        **more,
    )


def plane_call(stage, got, other, plane_tables):
    wire = (OWNERS, 8, SLOTS)
    cells = (PLANES, NG, LANES)
    share = (SHARE, LANES)
    shapes = {"first": (wire, cells), "next": (wire,), "last": (share, share)}[stage]
    scratch = [pltpu.VMEM((2 * PARTS * ROWS, OWNERS * SLOTS), BF16), pltpu.VMEM((CELLS, OWNERS * SLOTS), BF16)]
    operands, more = [got, other, *plane_tables], {}
    if stage == "last":
        operands.insert(2, lax.axis_index("core").reshape(1))
        whole = pl.BlockSpec(memory_space=pltpu.VMEM)
        specs = [whole] * len(operands)
        specs[2] = pl.BlockSpec(memory_space=pltpu.SMEM)
        more["in_specs"] = specs
    return call(functools.partial(plane_kernel, stage), "plane_" + stage, shapes, scratch, **more)(*operands)


def exchange(rows):
    return lax.all_to_all(rows, ("x", "z"), split_axis=0, concat_axis=0, tiled=True)


def swap(values, axis, mask):
    size = lax.axis_size(axis)
    return lax.ppermute(values, axis, [(s, s ^ mask) for s in range(size)])


def shards(psi, potential, stick_column, stick_length):
    stick_np, plane_np = tables()
    stick_table = jnp.asarray(stick_np)
    plane_tables = tuple(map(jnp.asarray, plane_np))
    wire, state = (OWNERS, 8, SLOTS), (SLOTS, LANES)
    weight = jnp.pad(potential.reshape(PLANES, NG, NG), ((0, 0), (0, 0), (0, LANES - NG)))
    term, kinetic, rows = call(start_kernel, "start", (state, state, wire))(
        psi.reshape(2, SLOTS, LANES), stick_column, stick_length, stick_table
    )
    total = term
    before = None
    psi_new = None
    for power in range(1, 4):
        got = exchange(rows)
        if power == 1:
            rows, before = plane_call("first", got, weight, plane_tables)
        else:
            (rows,) = plane_call("next", got, weight, plane_tables)
        got = exchange(rows)
        last = power == 3
        shapes = ((2, SLOTS, LANES), wire) if last else (state, state, wire)
        given = call(functools.partial(stick_kernel, power, last), f"stick_{power}", shapes)(
            got, term, total, kinetic, stick_column, stick_length, stick_table
        )
        if last:
            psi_new, rows = given
        else:
            term, total, rows = given
    keep, give = plane_call("last", exchange(rows), before, plane_tables)
    share = keep + swap(give, "core", 1)
    near, far, across = (swap(share, "y", mask) for mask in (1, 2, 3))
    share = (share + near) + (far + across)
    other = swap(share, "core", 1)
    mine = lax.axis_index("core") == 0
    change = jnp.concatenate([jnp.where(mine, share, other), jnp.where(mine, other, share)], axis=0)
    change = change.reshape(PLANES, NG, LANES)
    added = weight + LINEAR_GAIN * change + CUBIC_GAIN * change * change * change
    potential_new = added[:, :, :NG].reshape(PLANES, NG * NG)
    return psi_new.reshape(2, 1, SLOTS, LANES), potential_new


def solution(mesh):
    fine = Mesh(mesh.devices.reshape(4, 2, 4, 8), ("y", "core", "x", "z"))
    band, plane = ("y", "core"), ("x", "z")
    in_specs = (P(None, band, plane, None), P(plane, None), P(plane), P(plane))
    out_specs = (P(None, band, plane, None), P(plane, None))
    return jax.shard_map(shards, mesh=fine, in_specs=in_specs, out_specs=out_specs, check_vma=False)
```

```python
import functools
import math

import jax
import jax.numpy as jnp
import ml_dtypes
import numpy as np
from jax import lax
from jax.experimental import pallas as pl
from jax.experimental.pallas import tpu as pltpu
from jax.sharding import Mesh
from jax.sharding import PartitionSpec as P

NG = 96
RAD = 24
HALF = 64
LANES = 128
PLANES = 3
OWNERS = 32
SLOTS = 128
ROWS = 16
CHUNK = 4
CELLS = CHUNK * HALF
GROUP = 4
PARTS = 2 * PLANES
TIMESTEP = 0.6
LINEAR_GAIN = 0.5
CUBIC_GAIN = 0.3

F32 = jnp.float32
BF16 = jnp.bfloat16
NT = (((1,), (1,)), ((), ()))


def halves(values):
    high = values.astype(ml_dtypes.bfloat16)
    low = (values - high.astype(np.float64)).astype(ml_dtypes.bfloat16)
    return high, low


def wave(count, order):
    turns = np.outer(np.arange(count), np.arange(order) - RAD) % NG
    angle = turns * (2.0 * math.pi / NG)
    scale = NG**-0.5
    return np.cos(angle) * scale, np.sin(angle) * scale


def height_table():
    cosine, sine = wave(NG, 2 * RAD + 1)
    table = np.zeros((OWNERS, 8, LANES))
    order = 2 * RAD + 1
    for owner in range(OWNERS):
        for plane in range(PLANES):
            z = PLANES * owner + plane
            table[owner, 2 * plane, :order] = cosine[z]
            table[owner, 2 * plane, HALF : HALF + order] = -sine[z]
            table[owner, 2 * plane + 1, :order] = sine[z]
            table[owner, 2 * plane + 1, HALF : HALF + order] = cosine[z]
    return table.reshape(OWNERS * 8, LANES)


def second_table():
    cosine, sine = wave(NG, 2 * RAD + 1)
    order = 2 * RAD + 1
    table = np.zeros((LANES, 2 * LANES))
    table[:order, :NG] = cosine.T
    table[HALF : HALF + order, :NG] = -sine.T
    table[:order, LANES : LANES + NG] = sine.T
    table[HALF : HALF + order, LANES : LANES + NG] = cosine.T
    return table


def first_table():
    cosine, sine = wave(NG, 2 * RAD + 1)
    table = np.zeros((2 * NG, HALF))
    table[:NG, : 2 * RAD + 1] = cosine
    table[NG:, : 2 * RAD + 1] = sine
    return table


def tables():
    high, low = halves(height_table())
    order = np.arange(HALF)
    order = CHUNK * (order % ROWS) + order // ROWS
    second_high, second_low = halves(second_table())
    first = first_table()[:, order]
    first_high, first_low = halves(first)
    back = np.concatenate([first[:NG].T, first[NG:].T], axis=0)
    back_high, back_low = halves(back)
    stick = np.concatenate([high, low], axis=1)
    plane = (
        np.concatenate([second_high, second_high], axis=0),
        second_low,
        np.concatenate([first_high, first_low, first_high], axis=1),
        np.concatenate([back_high, back_low, back_high], axis=1),
        np.ascontiguousarray(second_high.T),
        np.ascontiguousarray(second_low.T),
    )
    return stick, plane


def split(values):
    high = values.astype(BF16)
    return high, (values - high.astype(F32)).astype(BF16)


def dot(left, right):
    return jnp.dot(left, right, preferred_element_type=F32)


def lanes_of(shape):
    return lax.broadcasted_iota(jnp.int32, shape, 1)


def signed_indices(column):
    first = jnp.floor((column + 0.5) * (1.0 / NG))
    second = column - NG * first
    first = jnp.where(first > NG // 2, first - NG, first)
    second = jnp.where(second > NG // 2, second - NG, second)
    return first + RAD, second + RAD


def cell_codes(first, second, length):
    row = jnp.floor((first + 0.5) * (1.0 / CHUNK))
    place = (first - CHUNK * row) * HALF + second
    live = length > 0.0
    return jnp.where(live, row, -1.0), jnp.where(live, place, -1.0)


def along_slots(row):
    return jnp.broadcast_to(row, (SLOTS, LANES)).T


def shift_lanes(values, amount, direction):
    for bit in range(5):
        step = 1 << bit
        moved = pltpu.roll(values, step if direction > 0 else LANES - step, 1)
        values = jnp.where((amount & step) != 0, moved, values)
    return values


def lane_shift(length_row):
    length = along_slots(length_row).astype(jnp.int32)
    return jnp.clip(RAD - ((length - 1) >> 1), 0, RAD), length


def send_heights(term, codes, stick_ref, out_ref):
    high, low = split(term)
    both = jnp.concatenate([high, low], axis=1)
    table_high, table_low = stick_ref[:, :LANES], stick_ref[:, LANES:]
    pair = jnp.concatenate([table_high, table_high], axis=1)
    rows = lax.dot_general(pair, both, NT, preferred_element_type=F32)
    rows = rows + lax.dot_general(table_low, high, NT, preferred_element_type=F32)
    rows = rows.reshape(OWNERS, 8, SLOTS)
    place = lax.broadcasted_iota(jnp.int32, (OWNERS, 8, SLOTS), 1)
    rows = jnp.where(place == 6, codes[0][None], rows)
    out_ref[...] = jnp.where(place == 7, codes[1][None], rows)


def slot_rows(column_ref, length_ref):
    column = column_ref[...].astype(F32).reshape(1, SLOTS)
    return column, length_ref[...].astype(F32).reshape(1, SLOTS)


def start_kernel(*refs):
    sources, (term_ref, kinetic_ref, out_ref) = refs[:4], refs[4:7]
    kept, arrived = refs[7:11], refs[11]
    copies = [pltpu.make_async_copy(*pair, arrived.at[n]) for n, pair in enumerate(zip(sources, kept))]
    for copy in copies:
        copy.start()
    psi_ref, column_ref, length_ref, stick_ref = kept
    copies[1].wait()
    copies[2].wait()
    column, length_row = slot_rows(column_ref, length_ref)
    first, second = signed_indices(column)
    codes = cell_codes(first, second, length_row)
    amount, length = lane_shift(length_row)
    lane = lanes_of((SLOTS, LANES))
    inside = lane < length
    copies[0].wait()
    real_part = shift_lanes(jnp.where(inside, psi_ref[0], 0.0), amount, 1)
    imag_part = shift_lanes(jnp.where(inside, psi_ref[1], 0.0), amount, 1)
    term = real_part + pltpu.roll(imag_part, HALF, 1)
    term_ref[...] = term
    depth = (lane & (HALF - 1)) - RAD
    spread = depth.astype(F32)
    first, second = first - RAD, second - RAD
    flat = along_slots(first * first + second * second)
    kinetic = (flat + spread * spread) / (RAD * RAD)
    valid = (jnp.abs(depth) <= ((length - 1) >> 1)) & (length > 0)
    kinetic_ref[...] = jnp.where(valid, kinetic, -1.0)
    copies[3].wait()
    send_heights(term, codes, stick_ref, out_ref)


def stick_kernel(power, last, *refs):
    got_ref, term_ref, total_ref, kinetic_ref, column_ref, length_ref, stick_ref = refs[:7]
    outs = refs[7:]
    out_ref = outs[-1]
    column, length_row = slot_rows(column_ref, length_ref)
    codes = cell_codes(*signed_indices(column), length_row)
    got = got_ref[...].reshape(OWNERS * 8, SLOTS).T
    high, low = split(got)
    back_high, back_low = stick_ref[:, :LANES], stick_ref[:, LANES:]
    applied = dot(high, back_high) + dot(low, back_high) + dot(high, back_low)
    kinetic = kinetic_ref[...]
    applied = jnp.where(kinetic >= 0.0, applied + kinetic * term_ref[...], 0.0)
    factor = TIMESTEP / power
    lane = lanes_of((SLOTS, LANES))
    term = pltpu.roll(applied, HALF, 1) * jnp.where(lane < HALF, factor, -factor)
    total = total_ref[...] + term
    outs[0][...] = total
    if last:
        send_heights(total, codes, stick_ref, out_ref)
    else:
        outs[1][...] = term
        send_heights(term, codes, stick_ref, out_ref)


def finish_kernel(total_ref, length_ref, psi_ref):
    total = total_ref[...]
    amount, _ = lane_shift(length_ref[...].astype(F32).reshape(1, SLOTS))
    lower = lanes_of((SLOTS, LANES)) < HALF
    psi_ref[0] = shift_lanes(jnp.where(lower, total, 0.0), amount, -1)
    psi_ref[1] = shift_lanes(jnp.where(lower, pltpu.roll(total, HALF, 1), 0.0), amount, -1)


def wide(row):
    return jnp.broadcast_to(row, (ROWS, SLOTS)).astype(BF16)


def cells_of(places):
    index = lax.broadcasted_iota(jnp.int32, (CELLS, SLOTS), 0).astype(BF16).reshape(CELLS // ROWS, ROWS, SLOTS)
    one, zero = jnp.ones((), BF16), jnp.zeros((), BF16)
    found = [jnp.where(index == wide(place)[None], one, zero).reshape(CELLS, SLOTS) for place in places]
    return jnp.concatenate(found, axis=1)


def plane_kernel(stage, *refs):
    refs = list(refs)
    got_ref = refs.pop(0)
    other_ref = refs.pop(0)
    second_pair, second_low, first_all, back_all, inner_high, inner_low = refs[:6]
    outs = refs[6:]
    row = lax.broadcasted_iota(jnp.int32, (ROWS, SLOTS), 0).astype(BF16)
    grids = [None, None]
    for group in range(OWNERS // GROUP):
        columns, places = [], []
        for owner in range(group * GROUP, (group + 1) * GROUP):
            got = got_ref[owner]
            high = got.astype(BF16).astype(F32)
            low = got - high
            mine = row == wide(got[6:7])
            zero = jnp.zeros((), BF16)
            parts = [jnp.where(mine, wide(part[r : r + 1]), zero) for part in (high, low) for r in range(PARTS)]
            columns.append(jnp.concatenate(parts, axis=0))
            places.append(got[7:8])
        spread = jnp.concatenate(columns, axis=1)
        cells = cells_of(places)
        for side in range(2):
            part = cells[side * LANES : (side + 1) * LANES]
            added = lax.dot_general(spread, part, NT, preferred_element_type=F32)
            grids[side] = added if grids[side] is None else grids[side] + added
    grid = jnp.concatenate(grids, axis=1)
    grid = (grid[: PARTS * ROWS] + grid[PARTS * ROWS :]).reshape(PLANES, 2, ROWS, CELLS)
    pieces = [
        jnp.concatenate([grid[:, part, :, c * HALF : (c + 1) * HALF] for part in range(2)], axis=2)
        for c in range(CHUNK)
    ]
    lined = jnp.stack(pieces, axis=1).reshape(PLANES * HALF, LANES)
    high, low = split(lined)
    middle = dot(jnp.concatenate([high, low], axis=1), second_pair[...]) + dot(high, second_low[...])
    returned = []
    for plane in range(PLANES):
        high, low = split(middle[plane * HALF : (plane + 1) * HALF])
        both = dot(first_all[...], jnp.concatenate([high, high, low], axis=0))
        real_part = both[:NG, :LANES] - both[NG:, LANES:]
        imag_part = both[NG:, :LANES] + both[:NG, LANES:]
        if stage == "first":
            outs[1][plane] = real_part * real_part + imag_part * imag_part
        if stage == "last":
            outs[0][plane] = real_part * real_part + imag_part * imag_part - other_ref[plane]
            continue
        weight = other_ref[plane]
        field = jnp.concatenate([real_part * weight, imag_part * weight], axis=1)
        high, low = split(field)
        both = dot(back_all[...], jnp.concatenate([high, high, low], axis=0))
        returned.append(
            jnp.concatenate(
                [both[:HALF, :LANES] + both[HALF:, LANES:], both[:HALF, LANES:] - both[HALF:, :LANES]],
                axis=1,
            )
        )
    if stage == "last":
        return
    high, low = split(jnp.concatenate(returned, axis=0))
    rows = dot(high, inner_high[...]) + dot(low, inner_high[...]) + dot(high, inner_low[...])
    rows = rows.reshape(PLANES, CHUNK, ROWS, LANES)
    pieces = [
        jnp.concatenate([rows[:, c, :, part * HALF : (part + 1) * HALF] for c in range(CHUNK)], axis=2)
        for part in range(2)
    ]
    high, low = split(jnp.stack(pieces, axis=1).reshape(PARTS * ROWS, CELLS))
    both = jnp.concatenate([high, low], axis=0)
    tail = jnp.zeros((2, SLOTS), F32)

    row = lax.broadcasted_iota(jnp.int32, (ROWS, SLOTS), 0).astype(F32)
    for owner in range(0, OWNERS, 2):
        pair = (owner, owner + 1)
        found = dot(both, cells_of([got_ref[o][7:8] for o in pair]))
        found = (found[: PARTS * ROWS] + found[PARTS * ROWS :]).reshape(PARTS, ROWS, 2 * SLOTS)
        for side, o in enumerate(pair):
            mine = row == got_ref[o][6:7]
            chosen = jnp.where(mine[None], found[:, :, side * SLOTS : (side + 1) * SLOTS], 0.0)
            outs[0][o] = jnp.concatenate([jnp.sum(chosen, axis=1), tail], axis=0)


def call(kernel, name, shapes, **more):
    return pl.pallas_call(
        kernel,
        **more,
        out_shape=tuple(jax.ShapeDtypeStruct(s, F32) for s in shapes),
        name=name,
        compiler_params=pltpu.CompilerParams(vmem_limit_bytes=32 << 20),
    )


def plane_call(stage, got, other, plane_tables):
    wire = (OWNERS, 8, SLOTS)
    cells = (PLANES, NG, LANES)
    shapes = {"first": (wire, cells), "next": (wire,), "last": (cells,)}[stage]
    return call(functools.partial(plane_kernel, stage), "plane_" + stage, shapes)(got, other, *plane_tables)


def exchange(rows):
    return lax.all_to_all(rows, ("x", "z"), split_axis=0, concat_axis=0, tiled=True)


def swap(values, axis, mask):
    size = lax.axis_size(axis)
    return lax.ppermute(values, axis, [(s, s ^ mask) for s in range(size)])


def shards(psi, potential, stick_column, stick_length):
    stick_np, plane_np = tables()
    stick_table = jnp.asarray(stick_np)
    plane_tables = tuple(map(jnp.asarray, plane_np))
    wire, state = (OWNERS, 8, SLOTS), (SLOTS, LANES)
    weight = jnp.pad(potential.reshape(PLANES, NG, NG), ((0, 0), (0, 0), (0, LANES - NG)))
    kept = (
        pltpu.VMEM((2, SLOTS, LANES), F32),
        pltpu.VMEM((SLOTS,), jnp.int32),
        pltpu.VMEM((SLOTS,), jnp.int32),
        pltpu.VMEM(stick_np.shape, BF16),
        pltpu.SemaphoreType.DMA((4,)),
    )
    begin = call(
        start_kernel,
        "start",
        (state, state, wire),
        in_specs=[pl.BlockSpec(memory_space=pltpu.HBM)] * 4,
        scratch_shapes=kept,
    )
    term, kinetic, rows = begin(
        *(
            pltpu.with_memory_space_constraint(source, pltpu.HBM)
            for source in (psi.reshape(2, SLOTS, LANES), stick_column, stick_length, stick_table)
        )
    )
    total = term
    before = None
    for power in range(1, 4):
        got = exchange(rows)
        if power == 1:
            rows, before = plane_call("first", got, weight, plane_tables)
        else:
            (rows,) = plane_call("next", got, weight, plane_tables)
        got = exchange(rows)
        last = power == 3
        shapes = (state, wire) if last else (state, state, wire)
        given = call(functools.partial(stick_kernel, power, last), f"stick_{power}", shapes)(
            got, term, total, kinetic, stick_column, stick_length, stick_table
        )
        if last:
            total, rows = given
        else:
            total, term, rows = given
    (change,) = plane_call("last", exchange(rows), before, plane_tables)
    near, far, across = (swap(change, "y", mask) for mask in (1, 2, 3))
    change = (change + near) + (far + across)
    change = change + swap(change, "core", 1)
    (psi_new,) = call(finish_kernel, "finish", ((2, SLOTS, LANES),))(total, stick_length)
    added = weight + LINEAR_GAIN * change + CUBIC_GAIN * change * change * change
    potential_new = added[:, :, :NG].reshape(PLANES, NG * NG)
    return psi_new.reshape(2, 1, SLOTS, LANES), potential_new


def solution(mesh):
    fine = Mesh(mesh.devices.reshape(4, 2, 4, 8), ("y", "core", "x", "z"))
    band, plane = ("y", "core"), ("x", "z")
    in_specs = (P(None, band, plane, None), P(plane, None), P(plane), P(plane))
    out_specs = (P(None, band, plane, None), P(plane, None))
    return jax.shard_map(shards, mesh=fine, in_specs=in_specs, out_specs=out_specs, check_vma=False)
```

```python
import functools
import math

import jax
import jax.numpy as jnp
import ml_dtypes
import numpy as np
from jax import lax
from jax.experimental import pallas as pl
from jax.experimental.pallas import tpu as pltpu
from jax.sharding import Mesh
from jax.sharding import PartitionSpec as P

NG = 96
RAD = 24
HALF = 64
LANES = 128
PLANES = 3
OWNERS = 32
SLOTS = 128
ROWS = 16
CHUNK = 4
CELLS = CHUNK * HALF
GROUP = 2
PARTS = 2 * PLANES
TIMESTEP = 0.6
LINEAR_GAIN = 0.5
CUBIC_GAIN = 0.3

F32 = jnp.float32
BF16 = jnp.bfloat16
NT = (((1,), (1,)), ((), ()))


def halves(values):
    high = values.astype(ml_dtypes.bfloat16)
    low = (values - high.astype(np.float64)).astype(ml_dtypes.bfloat16)
    return high, low


def wave(count, order):
    turns = np.outer(np.arange(count), np.arange(order) - RAD) % NG
    angle = turns * (2.0 * math.pi / NG)
    scale = NG**-0.5
    return np.cos(angle) * scale, np.sin(angle) * scale


def height_table():
    cosine, sine = wave(NG, 2 * RAD + 1)
    table = np.zeros((OWNERS, 8, LANES))
    order = 2 * RAD + 1
    for owner in range(OWNERS):
        for plane in range(PLANES):
            z = PLANES * owner + plane
            table[owner, 2 * plane, :order] = cosine[z]
            table[owner, 2 * plane, HALF : HALF + order] = -sine[z]
            table[owner, 2 * plane + 1, :order] = sine[z]
            table[owner, 2 * plane + 1, HALF : HALF + order] = cosine[z]
    return table.reshape(OWNERS * 8, LANES)


def second_table():
    cosine, sine = wave(NG, 2 * RAD + 1)
    order = 2 * RAD + 1
    table = np.zeros((LANES, 2 * LANES))
    table[:order, :NG] = cosine.T
    table[HALF : HALF + order, :NG] = -sine.T
    table[:order, LANES : LANES + NG] = sine.T
    table[HALF : HALF + order, LANES : LANES + NG] = cosine.T
    return table


def first_table():
    cosine, sine = wave(NG, 2 * RAD + 1)
    table = np.zeros((2 * NG, HALF))
    table[:NG, : 2 * RAD + 1] = cosine
    table[NG:, : 2 * RAD + 1] = sine
    return table


def tables():
    high, low = halves(height_table())
    order = np.arange(HALF)
    order = CHUNK * (order % ROWS) + order // ROWS
    second_high, second_low = halves(second_table())
    first = first_table()[:, order]
    first_high, first_low = halves(first)
    back = np.concatenate([first[:NG].T, first[NG:].T], axis=0)
    back_high, back_low = halves(back)
    stick = np.concatenate([high, low], axis=1)
    plane = (
        np.concatenate([second_high, second_high], axis=0),
        second_low,
        np.concatenate([first_high, first_low, first_high], axis=1),
        np.concatenate([back_high, back_low, back_high], axis=1),
        np.ascontiguousarray(second_high.T),
        np.ascontiguousarray(second_low.T),
    )
    return stick, plane


def split(values):
    high = values.astype(BF16)
    return high, (values - high.astype(F32)).astype(BF16)


def dot(left, right):
    return jnp.dot(left, right, preferred_element_type=F32)


def lanes_of(shape):
    return lax.broadcasted_iota(jnp.int32, shape, 1)


def signed_indices(column):
    first = jnp.floor((column + 0.5) * (1.0 / NG))
    second = column - NG * first
    first = jnp.where(first > NG // 2, first - NG, first)
    second = jnp.where(second > NG // 2, second - NG, second)
    return first + RAD, second + RAD


def cell_codes(first, second, length):
    row = jnp.floor((first + 0.5) * (1.0 / CHUNK))
    place = (first - CHUNK * row) * HALF + second
    live = length > 0.0
    return jnp.where(live, row, -1.0), jnp.where(live, place, -1.0)


def along_slots(row):
    return jnp.broadcast_to(row, (SLOTS, LANES)).T


def shift_lanes(values, amount, direction):
    for bit in range(5):
        step = 1 << bit
        moved = pltpu.roll(values, step if direction > 0 else LANES - step, 1)
        values = jnp.where((amount & step) != 0, moved, values)
    return values


def lane_shift(length_row):
    length = along_slots(length_row).astype(jnp.int32)
    return jnp.clip(RAD - ((length - 1) >> 1), 0, RAD), length


def send_heights(term, codes, stick_ref, out_ref):
    high, low = split(term)
    both = jnp.concatenate([high, low], axis=1)
    table_high, table_low = stick_ref[:, :LANES], stick_ref[:, LANES:]
    pair = jnp.concatenate([table_high, table_high], axis=1)
    rows = lax.dot_general(pair, both, NT, preferred_element_type=F32)
    rows = rows + lax.dot_general(table_low, high, NT, preferred_element_type=F32)
    rows = rows.reshape(OWNERS, 8, SLOTS)
    place = lax.broadcasted_iota(jnp.int32, (OWNERS, 8, SLOTS), 1)
    rows = jnp.where(place == 6, codes[0][None], rows)
    out_ref[...] = jnp.where(place == 7, codes[1][None], rows)


def slot_rows(column_ref, length_ref):
    column = column_ref[...].astype(F32).reshape(1, SLOTS)
    return column, length_ref[...].astype(F32).reshape(1, SLOTS)


def start_kernel(*refs):
    sources, (term_ref, kinetic_ref, places_ref, out_ref) = refs[:4], refs[4:8]
    kept, arrived = refs[8:12], refs[12]
    copies = [pltpu.make_async_copy(*pair, arrived.at[n]) for n, pair in enumerate(zip(sources, kept))]
    for copy in copies:
        copy.start()
    psi_ref, column_ref, length_ref, stick_ref = kept
    copies[1].wait()
    copies[2].wait()
    column, length_row = slot_rows(column_ref, length_ref)
    first, second = signed_indices(column)
    codes = cell_codes(first, second, length_row)
    amount, length = lane_shift(length_row)
    lane = lanes_of((SLOTS, LANES))
    inside = lane < length
    copies[0].wait()
    real_part = shift_lanes(jnp.where(inside, psi_ref[0], 0.0), amount, 1)
    imag_part = shift_lanes(jnp.where(inside, psi_ref[1], 0.0), amount, 1)
    term = real_part + pltpu.roll(imag_part, HALF, 1)
    term_ref[...] = term
    places_ref[...] = jnp.concatenate([*codes, length_row, jnp.zeros((5, SLOTS), F32)], axis=0)
    depth = (lane & (HALF - 1)) - RAD
    spread = depth.astype(F32)
    first, second = first - RAD, second - RAD
    flat = along_slots(first * first + second * second)
    kinetic = (flat + spread * spread) / (RAD * RAD)
    valid = (jnp.abs(depth) <= ((length - 1) >> 1)) & (length > 0)
    kinetic_ref[...] = jnp.where(valid, kinetic, -1.0)
    copies[3].wait()
    send_heights(term, codes, stick_ref, out_ref)


def stick_kernel(power, last, *refs):
    got_ref, term_ref, total_ref, kinetic_ref, places_ref, stick_ref = refs[:6]
    outs = refs[6:]
    out_ref = outs[-1]
    codes = places_ref[0:1], places_ref[1:2]
    got = got_ref[...].reshape(OWNERS * 8, SLOTS).T
    high, low = split(got)
    back_high, back_low = stick_ref[:, :LANES], stick_ref[:, LANES:]
    applied = dot(high, back_high) + dot(low, back_high) + dot(high, back_low)
    kinetic = kinetic_ref[...]
    applied = jnp.where(kinetic >= 0.0, applied + kinetic * term_ref[...], 0.0)
    factor = TIMESTEP / power
    lane = lanes_of((SLOTS, LANES))
    term = pltpu.roll(applied, HALF, 1) * jnp.where(lane < HALF, factor, -factor)
    total = total_ref[...] + term
    outs[0][...] = total
    if last:
        send_heights(total, codes, stick_ref, out_ref)
    else:
        outs[1][...] = term
        send_heights(term, codes, stick_ref, out_ref)


def finish_kernel(total_ref, places_ref, psi_ref):
    total = total_ref[...]
    amount, _ = lane_shift(places_ref[2:3])
    lower = lanes_of((SLOTS, LANES)) < HALF
    psi_ref[0] = shift_lanes(jnp.where(lower, total, 0.0), amount, -1)
    psi_ref[1] = shift_lanes(jnp.where(lower, pltpu.roll(total, HALF, 1), 0.0), amount, -1)


def wide(row):
    return jnp.broadcast_to(row, (ROWS, SLOTS)).astype(BF16)


def cells_of(places):
    index = lax.broadcasted_iota(jnp.int32, (CELLS, SLOTS), 0).astype(BF16).reshape(CELLS // ROWS, ROWS, SLOTS)
    one, zero = jnp.ones((), BF16), jnp.zeros((), BF16)
    found = [jnp.where(index == wide(place)[None], one, zero).reshape(CELLS, SLOTS) for place in places]
    return jnp.concatenate(found, axis=1)


def plane_kernel(stage, *refs):
    refs = list(refs)
    got_ref = refs.pop(0)
    other_ref = refs.pop(0)
    second_pair, second_low, first_all, back_all, inner_high, inner_low = refs[:6]
    outs = refs[6:]
    row = lax.broadcasted_iota(jnp.int32, (ROWS, SLOTS), 0).astype(BF16)
    grids = [None, None]
    for group in range(OWNERS // GROUP):
        columns, places = [], []
        for owner in range(group * GROUP, (group + 1) * GROUP):
            got = got_ref[owner]
            high = got.astype(BF16).astype(F32)
            low = got - high
            mine = row == wide(got[6:7])
            zero = jnp.zeros((), BF16)
            parts = [jnp.where(mine, wide(part[r : r + 1]), zero) for part in (high, low) for r in range(PARTS)]
            columns.append(jnp.concatenate(parts, axis=0))
            places.append(got[7:8])
        spread = jnp.concatenate(columns, axis=1)
        added = lax.dot_general(spread, cells_of(places), NT, preferred_element_type=F32)
        side = group % 2
        grids[side] = added if grids[side] is None else grids[side] + added
    grid = grids[0] + jnp.where(got_ref[0, 7:8, :1] > -2.0, grids[1], 0.0)
    grid = (grid[: PARTS * ROWS] + grid[PARTS * ROWS :]).reshape(PLANES, 2, ROWS, CELLS)
    pieces = [
        jnp.concatenate([grid[:, part, :, c * HALF : (c + 1) * HALF] for part in range(2)], axis=2)
        for c in range(CHUNK)
    ]
    lined = jnp.stack(pieces, axis=1).reshape(PLANES * HALF, LANES)
    high, low = split(lined)
    middle = dot(jnp.concatenate([high, low], axis=1), second_pair[...]) + dot(high, second_low[...])
    returned = []
    for plane in range(PLANES):
        high, low = split(middle[plane * HALF : (plane + 1) * HALF])
        both = dot(first_all[...], jnp.concatenate([high, high, low], axis=0))
        real_part = both[:NG, :LANES] - both[NG:, LANES:]
        imag_part = both[NG:, :LANES] + both[:NG, LANES:]
        if stage == "first":
            outs[1][plane] = real_part * real_part + imag_part * imag_part
        if stage == "last":
            outs[0][plane] = real_part * real_part + imag_part * imag_part - other_ref[plane]
            continue
        weight = other_ref[plane]
        field = jnp.concatenate([real_part * weight, imag_part * weight], axis=1)
        high, low = split(field)
        both = dot(back_all[...], jnp.concatenate([high, high, low], axis=0))
        returned.append(
            jnp.concatenate(
                [both[:HALF, :LANES] + both[HALF:, LANES:], both[:HALF, LANES:] - both[HALF:, :LANES]],
                axis=1,
            )
        )
    if stage == "last":
        return
    high, low = split(jnp.concatenate(returned, axis=0))
    rows = dot(high, inner_high[...]) + dot(low, inner_high[...]) + dot(high, inner_low[...])
    rows = rows.reshape(PLANES, CHUNK, ROWS, LANES)
    pieces = [
        jnp.concatenate([rows[:, c, :, part * HALF : (part + 1) * HALF] for c in range(CHUNK)], axis=2)
        for part in range(2)
    ]
    high, low = split(jnp.stack(pieces, axis=1).reshape(PARTS * ROWS, CELLS))
    both = jnp.concatenate([high, low], axis=0)
    tail = jnp.zeros((2, SLOTS), F32)

    row = lax.broadcasted_iota(jnp.int32, (ROWS, SLOTS), 0).astype(F32)
    for owner in range(0, OWNERS, 2):
        pair = (owner, owner + 1)
        found = dot(both, cells_of([got_ref[o][7:8] for o in pair]))
        found = (found[: PARTS * ROWS] + found[PARTS * ROWS :]).reshape(PARTS, ROWS, 2 * SLOTS)
        for side, o in enumerate(pair):
            mine = row == got_ref[o][6:7]
            chosen = jnp.where(mine[None], found[:, :, side * SLOTS : (side + 1) * SLOTS], 0.0)
            outs[0][o] = jnp.concatenate([jnp.sum(chosen, axis=1), tail], axis=0)


def call(kernel, name, shapes, **more):
    return pl.pallas_call(
        kernel,
        **more,
        out_shape=tuple(jax.ShapeDtypeStruct(s, F32) for s in shapes),
        name=name,
        compiler_params=pltpu.CompilerParams(vmem_limit_bytes=32 << 20),
    )


def plane_call(stage, got, other, plane_tables):
    wire = (OWNERS, 8, SLOTS)
    cells = (PLANES, NG, LANES)
    shapes = {"first": (wire, cells), "next": (wire,), "last": (cells,)}[stage]
    return call(functools.partial(plane_kernel, stage), "plane_" + stage, shapes)(got, other, *plane_tables)


def exchange(rows):
    return lax.all_to_all(rows, ("x", "z"), split_axis=0, concat_axis=0, tiled=True)


def swap(values, axis, mask):
    size = lax.axis_size(axis)
    return lax.ppermute(values, axis, [(s, s ^ mask) for s in range(size)])


def shards(psi, potential, stick_column, stick_length):
    stick_np, plane_np = tables()
    stick_table = jnp.asarray(stick_np)
    plane_tables = tuple(map(jnp.asarray, plane_np))
    wire, state = (OWNERS, 8, SLOTS), (SLOTS, LANES)
    weight = jnp.pad(potential.reshape(PLANES, NG, NG), ((0, 0), (0, 0), (0, LANES - NG)))
    kept = (
        pltpu.VMEM((2, SLOTS, LANES), F32),
        pltpu.VMEM((SLOTS,), jnp.int32),
        pltpu.VMEM((SLOTS,), jnp.int32),
        pltpu.VMEM(stick_np.shape, BF16),
        pltpu.SemaphoreType.DMA((4,)),
    )
    begin = call(
        start_kernel,
        "start",
        (state, state, (8, SLOTS), wire),
        in_specs=[pl.BlockSpec(memory_space=pltpu.HBM)] * 4,
        scratch_shapes=kept,
    )
    term, kinetic, places, rows = begin(
        *(
            pltpu.with_memory_space_constraint(source, pltpu.HBM)
            for source in (psi.reshape(2, SLOTS, LANES), stick_column, stick_length, stick_table)
        )
    )
    total = term
    before = None
    for power in range(1, 4):
        got = exchange(rows)
        if power == 1:
            rows, before = plane_call("first", got, weight, plane_tables)
        else:
            (rows,) = plane_call("next", got, weight, plane_tables)
        got = exchange(rows)
        last = power == 3
        shapes = (state, wire) if last else (state, state, wire)
        given = call(functools.partial(stick_kernel, power, last), f"stick_{power}", shapes)(
            got, term, total, kinetic, places, stick_table
        )
        if last:
            total, rows = given
        else:
            total, term, rows = given
    (change,) = plane_call("last", exchange(rows), before, plane_tables)
    near, far, across = (swap(change, "y", mask) for mask in (1, 2, 3))
    change = (change + near) + (far + across)
    change = change + swap(change, "core", 1)
    (psi_new,) = call(finish_kernel, "finish", ((2, SLOTS, LANES),))(total, places)
    added = weight + LINEAR_GAIN * change + CUBIC_GAIN * change * change * change
    potential_new = added[:, :, :NG].reshape(PLANES, NG * NG)
    return psi_new.reshape(2, 1, SLOTS, LANES), potential_new


def solution(mesh):
    fine = Mesh(mesh.devices.reshape(4, 2, 4, 8), ("y", "core", "x", "z"))
    band, plane = ("y", "core"), ("x", "z")
    in_specs = (P(None, band, plane, None), P(plane, None), P(plane), P(plane))
    out_specs = (P(None, band, plane, None), P(plane, None))
    return jax.shard_map(shards, mesh=fine, in_specs=in_specs, out_specs=out_specs, check_vma=False)
```

```python
import functools
import math

import jax
import jax.numpy as jnp
import ml_dtypes
import numpy as np
from jax import lax
from jax.experimental import pallas as pl
from jax.experimental.pallas import tpu as pltpu
from jax.sharding import Mesh
from jax.sharding import PartitionSpec as P

NG = 96
RAD = 24
HALF = 64
LANES = 128
PLANES = 3
OWNERS = 32
SLOTS = 128
ROWS = 16
CHUNK = 4
CELLS = CHUNK * HALF
GROUP = 2
FLAT = NG * NG // LANES
PARTS = 2 * PLANES
TIMESTEP = 0.6
LINEAR_GAIN = 0.5
CUBIC_GAIN = 0.3

F32 = jnp.float32
BF16 = jnp.bfloat16
NT = (((1,), (1,)), ((), ()))


def halves(values):
    high = values.astype(ml_dtypes.bfloat16)
    low = (values - high.astype(np.float64)).astype(ml_dtypes.bfloat16)
    return high, low


def wave(count, order):
    turns = np.outer(np.arange(count), np.arange(order) - RAD) % NG
    angle = turns * (2.0 * math.pi / NG)
    scale = NG**-0.5
    return np.cos(angle) * scale, np.sin(angle) * scale


def height_table():
    cosine, sine = wave(NG, 2 * RAD + 1)
    table = np.zeros((OWNERS, 8, LANES))
    order = 2 * RAD + 1
    for owner in range(OWNERS):
        for plane in range(PLANES):
            z = PLANES * owner + plane
            table[owner, 2 * plane, :order] = cosine[z]
            table[owner, 2 * plane, HALF : HALF + order] = -sine[z]
            table[owner, 2 * plane + 1, :order] = sine[z]
            table[owner, 2 * plane + 1, HALF : HALF + order] = cosine[z]
    return table.reshape(OWNERS * 8, LANES)


def second_table():
    cosine, sine = wave(NG, 2 * RAD + 1)
    order = 2 * RAD + 1
    table = np.zeros((LANES, 2 * LANES))
    table[:order, :NG] = cosine.T
    table[HALF : HALF + order, :NG] = -sine.T
    table[:order, LANES : LANES + NG] = sine.T
    table[HALF : HALF + order, LANES : LANES + NG] = cosine.T
    return table


def first_table():
    cosine, sine = wave(NG, 2 * RAD + 1)
    table = np.zeros((2 * NG, HALF))
    table[:NG, : 2 * RAD + 1] = cosine
    table[NG:, : 2 * RAD + 1] = sine
    return table


def tables():
    high, low = halves(height_table())
    order = np.arange(HALF)
    order = CHUNK * (order % ROWS) + order // ROWS
    second_high, second_low = halves(second_table())
    first = first_table()[:, order]
    first_high, first_low = halves(first)
    back = np.concatenate([first[:NG].T, first[NG:].T], axis=0)
    back_high, back_low = halves(back)
    stick = np.concatenate([high, low], axis=1)
    plane = (
        np.concatenate([second_high, second_high], axis=0),
        second_low,
        np.concatenate([first_high, first_low, first_high], axis=1),
        np.concatenate([back_high, back_low, back_high], axis=1),
        np.ascontiguousarray(second_high.T),
        np.ascontiguousarray(second_low.T),
    )
    return stick, plane


def split(values):
    high = values.astype(BF16)
    return high, (values - high.astype(F32)).astype(BF16)


def dot(left, right):
    return jnp.dot(left, right, preferred_element_type=F32)


def lanes_of(shape):
    return lax.broadcasted_iota(jnp.int32, shape, 1)


def signed_indices(column):
    first = jnp.floor((column + 0.5) * (1.0 / NG))
    second = column - NG * first
    first = jnp.where(first > NG // 2, first - NG, first)
    second = jnp.where(second > NG // 2, second - NG, second)
    return first + RAD, second + RAD


def cell_codes(first, second, length):
    row = jnp.floor((first + 0.5) * (1.0 / CHUNK))
    place = (first - CHUNK * row) * HALF + second
    live = length > 0.0
    return jnp.where(live, row, -1.0), jnp.where(live, place, -1.0)


def along_slots(row):
    return jnp.broadcast_to(row, (SLOTS, LANES)).T


def shift_lanes(values, amount, direction):
    for bit in range(5):
        step = 1 << bit
        moved = pltpu.roll(values, step if direction > 0 else LANES - step, 1)
        values = jnp.where((amount & step) != 0, moved, values)
    return values


def lane_shift(length_row):
    length = along_slots(length_row).astype(jnp.int32)
    return jnp.clip(RAD - ((length - 1) >> 1), 0, RAD), length


def send_heights(term, codes, stick_ref, out_ref):
    high, low = split(term)
    both = jnp.concatenate([high, low], axis=1)
    table_high, table_low = stick_ref[:, :LANES], stick_ref[:, LANES:]
    pair = jnp.concatenate([table_high, table_high], axis=1)
    rows = lax.dot_general(pair, both, NT, preferred_element_type=F32)
    rows = rows + lax.dot_general(table_low, high, NT, preferred_element_type=F32)
    rows = rows.reshape(OWNERS, 8, SLOTS)
    place = lax.broadcasted_iota(jnp.int32, (OWNERS, 8, SLOTS), 1)
    rows = jnp.where(place == 6, codes[0][None], rows)
    out_ref[...] = jnp.where(place == 7, codes[1][None], rows)


def slot_rows(column_ref, length_ref):
    column = column_ref[...].astype(F32).reshape(1, SLOTS)
    return column, length_ref[...].astype(F32).reshape(1, SLOTS)


def start_kernel(*refs):
    sources, (term_ref, kinetic_ref, places_ref, out_ref) = refs[:5], refs[5:9]
    kept, arrived = (*refs[10:14], refs[9]), refs[14]
    copies = [pltpu.make_async_copy(*pair, arrived.at[n]) for n, pair in enumerate(zip(sources, kept))]
    for copy in copies:
        copy.start()
    psi_ref, column_ref, length_ref, stick_ref = kept[:4]
    copies[1].wait()
    copies[2].wait()
    column, length_row = slot_rows(column_ref, length_ref)
    first, second = signed_indices(column)
    codes = cell_codes(first, second, length_row)
    amount, length = lane_shift(length_row)
    lane = lanes_of((SLOTS, LANES))
    places_ref[...] = jnp.concatenate([*codes, length_row, jnp.zeros((5, SLOTS), F32)], axis=0)
    depth = (lane & (HALF - 1)) - RAD
    spread = depth.astype(F32)
    first, second = first - RAD, second - RAD
    flat = along_slots(first * first + second * second)
    kinetic = (flat + spread * spread) / (RAD * RAD)
    valid = (jnp.abs(depth) <= ((length - 1) >> 1)) & (length > 0)
    kinetic_ref[...] = jnp.where(valid, kinetic, -1.0)
    inside = lane < length
    copies[0].wait()
    real_part = shift_lanes(jnp.where(inside, psi_ref[0], 0.0), amount, 1)
    imag_part = shift_lanes(jnp.where(inside, psi_ref[1], 0.0), amount, 1)
    term = real_part + pltpu.roll(imag_part, HALF, 1)
    term_ref[...] = term
    copies[3].wait()
    send_heights(term, codes, stick_ref, out_ref)
    copies[4].wait()


def stick_kernel(power, last, *refs):
    got_ref, term_ref, total_ref, kinetic_ref, places_ref, stick_ref = refs[:6]
    outs = refs[6:]
    out_ref = outs[-1]
    codes = places_ref[0:1], places_ref[1:2]
    got = got_ref[...].reshape(OWNERS * 8, SLOTS).T
    high, low = split(got)
    back_high, back_low = stick_ref[:, :LANES], stick_ref[:, LANES:]
    applied = dot(high, back_high) + dot(low, back_high) + dot(high, back_low)
    kinetic = kinetic_ref[...]
    applied = jnp.where(kinetic >= 0.0, applied + kinetic * term_ref[...], 0.0)
    factor = TIMESTEP / power
    lane = lanes_of((SLOTS, LANES))
    term = pltpu.roll(applied, HALF, 1) * jnp.where(lane < HALF, factor, -factor)
    total = total_ref[...] + term
    outs[0][...] = total
    if last:
        send_heights(total, codes, stick_ref, out_ref)
    else:
        outs[1][...] = term
        send_heights(term, codes, stick_ref, out_ref)


def finish_kernel(total_ref, places_ref, psi_ref):
    total = total_ref[...]
    amount, _ = lane_shift(places_ref[2:3])
    lower = lanes_of((SLOTS, LANES)) < HALF
    psi_ref[0] = shift_lanes(jnp.where(lower, total, 0.0), amount, -1)
    psi_ref[1] = shift_lanes(jnp.where(lower, pltpu.roll(total, HALF, 1), 0.0), amount, -1)


def wide(row):
    return jnp.broadcast_to(row, (ROWS, SLOTS)).astype(BF16)


def cells_of(places):
    index = lax.broadcasted_iota(jnp.int32, (CELLS, SLOTS), 0).astype(BF16).reshape(CELLS // ROWS, ROWS, SLOTS)
    one, zero = jnp.ones((), BF16), jnp.zeros((), BF16)
    found = [jnp.where(index == wide(place)[None], one, zero).reshape(CELLS, SLOTS) for place in places]
    return jnp.concatenate(found, axis=1)


def pack_cells(cells_ref, flat_ref, start):
    lane = lanes_of((NG // CHUNK, LANES))
    rows = [cells_ref[pl.ds(c, NG // CHUNK, stride=CHUNK), :] for c in range(CHUNK)]
    rows = [rows[0], *(pltpu.roll(rows[c], LANES - 32 * c, 1) for c in range(1, CHUNK))]
    for c in range(CHUNK - 1):
        kept = jnp.where(lane < NG - 32 * c, rows[c], rows[c + 1])
        flat_ref[pl.ds(start + c, NG // CHUNK, stride=CHUNK - 1), :] = kept


def unpack_cells(line_ref, flat_ref, cells_ref):
    for plane in range(PLANES):
        for k in range(FLAT):
            flat_ref[plane * FLAT + k : plane * FLAT + k + 1, :] = line_ref[
                plane : plane + 1, k * LANES : (k + 1) * LANES
            ]
    lane = lanes_of((NG // CHUNK, LANES))
    for plane in range(PLANES):
        parts = [
            flat_ref[pl.ds(plane * FLAT + v, NG // CHUNK, stride=CHUNK - 1), :] for v in range(CHUNK - 1)
        ]
        for c in range(CHUNK):
            if c in (0, CHUNK - 1):
                both = parts[min(c, CHUNK - 2)]
            else:
                both = jnp.where(lane < NG - 32 * c, parts[c], parts[c - 1])
            both = pltpu.roll(both, 32 * c, 1) if c else both
            cells_ref[pl.ds(plane * NG + c, NG // CHUNK, stride=CHUNK), :] = jnp.where(lane < NG, both, 0.0)


def plane_kernel(stage, *refs):
    refs = list(refs)
    got_ref = refs.pop(0)
    other_ref = refs.pop(0)
    second_pair, second_low, first_all, back_all, inner_high, inner_low = refs[:6]
    outs = refs[6:]
    weight_ref = other_ref
    if stage == "first":
        weight_ref = outs[2]
        unpack_cells(other_ref, outs[3], weight_ref)
    row = lax.broadcasted_iota(jnp.int32, (ROWS, SLOTS), 0).astype(BF16)
    grids = [None, None]
    for group in range(OWNERS // GROUP):
        columns, places = [], []
        for owner in range(group * GROUP, (group + 1) * GROUP):
            got = got_ref[owner]
            high = got.astype(BF16).astype(F32)
            low = got - high
            mine = row == wide(got[6:7])
            zero = jnp.zeros((), BF16)
            parts = [jnp.where(mine, wide(part[r : r + 1]), zero) for part in (high, low) for r in range(PARTS)]
            columns.append(jnp.concatenate(parts, axis=0))
            places.append(got[7:8])
        spread = jnp.concatenate(columns, axis=1)
        added = lax.dot_general(spread, cells_of(places), NT, preferred_element_type=F32)
        side = group % 2
        grids[side] = added if grids[side] is None else grids[side] + added
    grid = grids[0] + jnp.where(got_ref[0, 7:8, :1] > -2.0, grids[1], 0.0)
    grid = (grid[: PARTS * ROWS] + grid[PARTS * ROWS :]).reshape(PLANES, 2, ROWS, CELLS)
    pieces = [
        jnp.concatenate([grid[:, part, :, c * HALF : (c + 1) * HALF] for part in range(2)], axis=2)
        for c in range(CHUNK)
    ]
    lined = jnp.stack(pieces, axis=1).reshape(PLANES * HALF, LANES)
    high, low = split(lined)
    middle = dot(jnp.concatenate([high, low], axis=1), second_pair[...]) + dot(high, second_low[...])
    returned = []
    for plane in range(PLANES):
        high, low = split(middle[plane * HALF : (plane + 1) * HALF])
        both = dot(first_all[...], jnp.concatenate([high, high, low], axis=0))
        real_part = both[:NG, :LANES] - both[NG:, LANES:]
        imag_part = both[NG:, :LANES] + both[:NG, LANES:]
        if stage == "first":
            outs[1][plane] = real_part * real_part + imag_part * imag_part
        if stage == "last":
            outs[1][...] = real_part * real_part + imag_part * imag_part - other_ref[plane]
            pack_cells(outs[1], outs[0], plane * FLAT)
            continue
        weight = weight_ref[plane * NG : (plane + 1) * NG]
        field = jnp.concatenate([real_part * weight, imag_part * weight], axis=1)
        high, low = split(field)
        both = dot(back_all[...], jnp.concatenate([high, high, low], axis=0))
        returned.append(
            jnp.concatenate(
                [both[:HALF, :LANES] + both[HALF:, LANES:], both[:HALF, LANES:] - both[HALF:, :LANES]],
                axis=1,
            )
        )
    if stage == "last":
        return
    high, low = split(jnp.concatenate(returned, axis=0))
    rows = dot(high, inner_high[...]) + dot(low, inner_high[...]) + dot(high, inner_low[...])
    rows = rows.reshape(PLANES, CHUNK, ROWS, LANES)
    pieces = [
        jnp.concatenate([rows[:, c, :, part * HALF : (part + 1) * HALF] for c in range(CHUNK)], axis=2)
        for part in range(2)
    ]
    high, low = split(jnp.stack(pieces, axis=1).reshape(PARTS * ROWS, CELLS))
    both = jnp.concatenate([high, low], axis=0)
    tail = jnp.zeros((2, SLOTS), F32)

    row = lax.broadcasted_iota(jnp.int32, (ROWS, SLOTS), 0).astype(F32)
    for owner in range(0, OWNERS, 2):
        pair = (owner, owner + 1)
        found = dot(both, cells_of([got_ref[o][7:8] for o in pair]))
        found = (found[: PARTS * ROWS] + found[PARTS * ROWS :]).reshape(PARTS, ROWS, 2 * SLOTS)
        for side, o in enumerate(pair):
            mine = row == got_ref[o][6:7]
            chosen = jnp.where(mine[None], found[:, :, side * SLOTS : (side + 1) * SLOTS], 0.0)
            outs[0][o] = jnp.concatenate([jnp.sum(chosen, axis=1), tail], axis=0)


def call(kernel, name, shapes, **more):
    return pl.pallas_call(
        kernel,
        **more,
        out_shape=tuple(jax.ShapeDtypeStruct(s, F32) for s in shapes),
        name=name,
        compiler_params=pltpu.CompilerParams(vmem_limit_bytes=32 << 20),
    )


def plane_call(stage, got, other, plane_tables):
    wire = (OWNERS, 8, SLOTS)
    cells = (PLANES, NG, LANES)
    shapes = {"first": (wire, cells, (PLANES * NG, LANES), (PLANES * FLAT, LANES)), "next": (wire,), "last": ((PLANES * FLAT, LANES),)}[stage]
    more = {"scratch_shapes": [pltpu.VMEM((NG, LANES), F32)]} if stage == "last" else {}
    return call(functools.partial(plane_kernel, stage), "plane_" + stage, shapes, **more)(got, other, *plane_tables)


def exchange(rows):
    return lax.all_to_all(rows, ("x", "z"), split_axis=0, concat_axis=0, tiled=True)


def swap(values, axis, mask):
    size = lax.axis_size(axis)
    return lax.ppermute(values, axis, [(s, s ^ mask) for s in range(size)])


def shards(psi, potential, stick_column, stick_length):
    stick_np, plane_np = tables()
    stick_table = jnp.asarray(stick_np)
    plane_tables = tuple(map(jnp.asarray, plane_np))
    wire, state = (OWNERS, 8, SLOTS), (SLOTS, LANES)
    kept = (
        pltpu.VMEM((2, SLOTS, LANES), F32),
        pltpu.VMEM((SLOTS,), jnp.int32),
        pltpu.VMEM((SLOTS,), jnp.int32),
        pltpu.VMEM(stick_np.shape, BF16),
        pltpu.SemaphoreType.DMA((5,)),
    )
    begin = call(
        start_kernel,
        "start",
        (state, state, (8, SLOTS), wire, potential.shape),
        in_specs=[pl.BlockSpec(memory_space=pltpu.HBM)] * 5,
        scratch_shapes=kept,
    )
    term, kinetic, places, rows, kept_potential = begin(
        *(
            pltpu.with_memory_space_constraint(source, pltpu.HBM)
            for source in (psi.reshape(2, SLOTS, LANES), stick_column, stick_length, stick_table, potential)
        )
    )
    total = term
    before = weight = flat = None
    for power in range(1, 4):
        got = exchange(rows)
        if power == 1:
            rows, before, weight, flat = plane_call("first", got, kept_potential, plane_tables)
        else:
            (rows,) = plane_call("next", got, weight, plane_tables)
        got = exchange(rows)
        last = power == 3
        shapes = (state, wire) if last else (state, state, wire)
        given = call(functools.partial(stick_kernel, power, last), f"stick_{power}", shapes)(
            got, term, total, kinetic, places, stick_table
        )
        if last:
            total, rows = given
        else:
            total, term, rows = given
    (change,) = plane_call("last", exchange(rows), before, plane_tables)
    near, far, across = (swap(change, "y", mask) for mask in (1, 2, 3))
    (psi_new,) = call(finish_kernel, "finish", ((2, SLOTS, LANES),))(total, places)
    change = (change + near) + (far + across)
    change = change + swap(change, "core", 1)
    added = flat + LINEAR_GAIN * change + CUBIC_GAIN * change * change * change
    return psi_new.reshape(2, 1, SLOTS, LANES), added.reshape(PLANES, NG * NG)


def solution(mesh):
    fine = Mesh(mesh.devices.reshape(4, 2, 4, 8), ("y", "core", "x", "z"))
    band, plane = ("y", "core"), ("x", "z")
    in_specs = (P(None, band, plane, None), P(plane, None), P(plane), P(plane))
    out_specs = (P(None, band, plane, None), P(plane, None))
    return jax.shard_map(shards, mesh=fine, in_specs=in_specs, out_specs=out_specs, check_vma=False)
```

```python
import functools
import math

import jax
import jax.numpy as jnp
import ml_dtypes
import numpy as np
from jax import lax
from jax.experimental import pallas as pl
from jax.experimental.pallas import tpu as pltpu
from jax.sharding import Mesh
from jax.sharding import PartitionSpec as P

NG = 96
RAD = 24
HALF = 64
LANES = 128
PLANES = 3
OWNERS = 32
SLOTS = 128
ROWS = 16
CHUNK = 4
CELLS = CHUNK * HALF
GROUP = 2
FLAT = NG * NG // LANES
PARTS = 2 * PLANES
TIMESTEP = 0.6
LINEAR_GAIN = 0.5
CUBIC_GAIN = 0.3

F32 = jnp.float32
BF16 = jnp.bfloat16
NT = (((1,), (1,)), ((), ()))


def halves(values):
    high = values.astype(ml_dtypes.bfloat16)
    low = (values - high.astype(np.float64)).astype(ml_dtypes.bfloat16)
    return high, low


def wave(count, order):
    turns = np.outer(np.arange(count), np.arange(order) - RAD) % NG
    angle = turns * (2.0 * math.pi / NG)
    scale = NG**-0.5
    return np.cos(angle) * scale, np.sin(angle) * scale


def height_table():
    cosine, sine = wave(NG, 2 * RAD + 1)
    table = np.zeros((OWNERS, 8, LANES))
    order = 2 * RAD + 1
    for owner in range(OWNERS):
        for plane in range(PLANES):
            z = PLANES * owner + plane
            table[owner, 2 * plane, :order] = cosine[z]
            table[owner, 2 * plane, HALF : HALF + order] = -sine[z]
            table[owner, 2 * plane + 1, :order] = sine[z]
            table[owner, 2 * plane + 1, HALF : HALF + order] = cosine[z]
    return table.reshape(OWNERS * 8, LANES)


def second_table():
    cosine, sine = wave(NG, 2 * RAD + 1)
    order = 2 * RAD + 1
    table = np.zeros((LANES, 2 * LANES))
    table[:order, :NG] = cosine.T
    table[HALF : HALF + order, :NG] = -sine.T
    table[:order, LANES : LANES + NG] = sine.T
    table[HALF : HALF + order, LANES : LANES + NG] = cosine.T
    return table


def first_table():
    cosine, sine = wave(NG, 2 * RAD + 1)
    table = np.zeros((2 * NG, HALF))
    table[:NG, : 2 * RAD + 1] = cosine
    table[NG:, : 2 * RAD + 1] = sine
    return table


def tables():
    high, low = halves(height_table())
    order = np.arange(HALF)
    order = CHUNK * (order % ROWS) + order // ROWS
    second_high, second_low = halves(second_table())
    first = first_table()[:, order]
    first_high, first_low = halves(first)
    back = np.concatenate([first[:NG].T, first[NG:].T], axis=0)
    back_high, back_low = halves(back)
    stick = np.concatenate([high, low], axis=1)
    plane = (
        np.concatenate([second_high, second_high], axis=0),
        second_low,
        np.concatenate([first_high, first_low, first_high], axis=1),
        np.concatenate([back_high, back_low, back_high], axis=1),
        np.ascontiguousarray(second_high.T),
        np.ascontiguousarray(second_low.T),
    )
    return stick, plane


def split(values):
    high = values.astype(BF16)
    return high, (values - high.astype(F32)).astype(BF16)


def dot(left, right):
    return jnp.dot(left, right, preferred_element_type=F32)


def lanes_of(shape):
    return lax.broadcasted_iota(jnp.int32, shape, 1)


def signed_indices(column):
    first = jnp.floor((column + 0.5) * (1.0 / NG))
    second = column - NG * first
    first = jnp.where(first > NG // 2, first - NG, first)
    second = jnp.where(second > NG // 2, second - NG, second)
    return first + RAD, second + RAD


def cell_codes(first, second, length):
    row = jnp.floor((first + 0.5) * (1.0 / CHUNK))
    place = (first - CHUNK * row) * HALF + second
    live = length > 0.0
    return jnp.where(live, row, -1.0), jnp.where(live, place, -1.0)


def along_slots(row):
    return jnp.broadcast_to(row, (SLOTS, LANES)).T


def shift_lanes(values, amount, direction):
    for bit in range(5):
        step = 1 << bit
        moved = pltpu.roll(values, step if direction > 0 else LANES - step, 1)
        values = jnp.where((amount & step) != 0, moved, values)
    return values


def lane_shift(length_row):
    length = along_slots(length_row).astype(jnp.int32)
    return jnp.clip(RAD - ((length - 1) >> 1), 0, RAD), length


def send_heights(term, codes, stick_ref, out_ref):
    high, low = split(term)
    both = jnp.concatenate([high, low], axis=1)
    table_high, table_low = stick_ref[:, :LANES], stick_ref[:, LANES:]
    pair = jnp.concatenate([table_high, table_high], axis=1)
    rows = lax.dot_general(pair, both, NT, preferred_element_type=F32)
    rows = rows + lax.dot_general(table_low, high, NT, preferred_element_type=F32)
    rows = rows.reshape(OWNERS, 8, SLOTS)
    place = lax.broadcasted_iota(jnp.int32, (OWNERS, 8, SLOTS), 1)
    rows = jnp.where(place == 6, codes[0][None], rows)
    out_ref[...] = jnp.where(place == 7, codes[1][None], rows)


def slot_rows(column_ref, length_ref):
    column = column_ref[...].astype(F32).reshape(1, SLOTS)
    return column, length_ref[...].astype(F32).reshape(1, SLOTS)


def start_kernel(*refs):
    sources, (term_ref, kinetic_ref, places_ref, out_ref) = refs[:5], refs[5:9]
    kept, arrived = (*refs[10:14], refs[9]), refs[14]
    copies = [pltpu.make_async_copy(*pair, arrived.at[n]) for n, pair in enumerate(zip(sources, kept))]
    for copy in copies:
        copy.start()
    psi_ref, column_ref, length_ref, stick_ref = kept[:4]
    copies[1].wait()
    copies[2].wait()
    column, length_row = slot_rows(column_ref, length_ref)
    first, second = signed_indices(column)
    codes = cell_codes(first, second, length_row)
    amount, length = lane_shift(length_row)
    lane = lanes_of((SLOTS, LANES))
    places_ref[...] = jnp.concatenate([*codes, length_row, jnp.zeros((5, SLOTS), F32)], axis=0)
    depth = (lane & (HALF - 1)) - RAD
    spread = depth.astype(F32)
    first, second = first - RAD, second - RAD
    flat = along_slots(first * first + second * second)
    kinetic = (flat + spread * spread) / (RAD * RAD)
    valid = (jnp.abs(depth) <= ((length - 1) >> 1)) & (length > 0)
    kinetic_ref[...] = jnp.where(valid, kinetic, -1.0)
    inside = lane < length
    copies[0].wait()
    real_part = jnp.where(inside, psi_ref[0], 0.0)
    imag_part = jnp.where(inside, psi_ref[1], 0.0)
    term = shift_lanes(real_part + pltpu.roll(imag_part, HALF, 1), amount, 1)
    term_ref[...] = term
    copies[3].wait()
    send_heights(term, codes, stick_ref, out_ref)
    copies[4].wait()


def stick_kernel(power, last, *refs):
    got_ref, term_ref, total_ref, kinetic_ref, places_ref, stick_ref = refs[:6]
    outs = refs[6:]
    out_ref = outs[-1]
    codes = places_ref[0:1], places_ref[1:2]
    got = got_ref[...].reshape(OWNERS * 8, SLOTS).T
    high, low = split(got)
    back_high, back_low = stick_ref[:, :LANES], stick_ref[:, LANES:]
    applied = dot(high, back_high) + dot(low, back_high) + dot(high, back_low)
    kinetic = kinetic_ref[...]
    applied = jnp.where(kinetic >= 0.0, applied + kinetic * term_ref[...], 0.0)
    factor = TIMESTEP / power
    lane = lanes_of((SLOTS, LANES))
    term = pltpu.roll(applied, HALF, 1) * jnp.where(lane < HALF, factor, -factor)
    total = total_ref[...] + term
    outs[0][...] = total
    if last:
        send_heights(total, codes, stick_ref, out_ref)
    else:
        outs[1][...] = term
        send_heights(term, codes, stick_ref, out_ref)


def finish_kernel(total_ref, places_ref, psi_ref):
    amount, _ = lane_shift(places_ref[2:3])
    total = shift_lanes(total_ref[...], amount, -1)
    lower = lanes_of((SLOTS, LANES)) < HALF
    psi_ref[0] = jnp.where(lower, total, 0.0)
    psi_ref[1] = jnp.where(lower, pltpu.roll(total, HALF, 1), 0.0)


def wide(row):
    return jnp.broadcast_to(row, (ROWS, SLOTS)).astype(BF16)


def cells_of(places):
    index = lax.broadcasted_iota(jnp.int32, (CELLS, SLOTS), 0).astype(BF16).reshape(CELLS // ROWS, ROWS, SLOTS)
    one, zero = jnp.ones((), BF16), jnp.zeros((), BF16)
    found = [jnp.where(index == wide(place)[None], one, zero).reshape(CELLS, SLOTS) for place in places]
    return jnp.concatenate(found, axis=1)


def pack_cells(cells_ref, flat_ref, start):
    lane = lanes_of((NG // CHUNK, LANES))
    rows = [cells_ref[pl.ds(c, NG // CHUNK, stride=CHUNK), :] for c in range(CHUNK)]
    rows = [rows[0], *(pltpu.roll(rows[c], LANES - 32 * c, 1) for c in range(1, CHUNK))]
    for c in range(CHUNK - 1):
        kept = jnp.where(lane < NG - 32 * c, rows[c], rows[c + 1])
        flat_ref[pl.ds(start + c, NG // CHUNK, stride=CHUNK - 1), :] = kept


def unpack_cells(line_ref, flat_ref, cells_ref):
    for plane in range(PLANES):
        for k in range(FLAT):
            flat_ref[plane * FLAT + k : plane * FLAT + k + 1, :] = line_ref[
                plane : plane + 1, k * LANES : (k + 1) * LANES
            ]
    lane = lanes_of((NG // CHUNK, LANES))
    for plane in range(PLANES):
        parts = [
            flat_ref[pl.ds(plane * FLAT + v, NG // CHUNK, stride=CHUNK - 1), :] for v in range(CHUNK - 1)
        ]
        for c in range(CHUNK):
            if c in (0, CHUNK - 1):
                both = parts[min(c, CHUNK - 2)]
            else:
                both = jnp.where(lane < NG - 32 * c, parts[c], parts[c - 1])
            both = pltpu.roll(both, 32 * c, 1) if c else both
            cells_ref[pl.ds(plane * NG + c, NG // CHUNK, stride=CHUNK), :] = jnp.where(lane < NG, both, 0.0)


def plane_kernel(stage, *refs):
    refs = list(refs)
    got_ref = refs.pop(0)
    other_ref = refs.pop(0)
    second_pair, second_low, first_all, back_all, inner_high, inner_low = refs[:6]
    outs = refs[6:]
    weight_ref = other_ref
    if stage == "first":
        weight_ref = outs[2]
        unpack_cells(other_ref, outs[3], weight_ref)
    row = lax.broadcasted_iota(jnp.int32, (ROWS, SLOTS), 0).astype(BF16)
    grids = [None, None]
    for group in range(OWNERS // GROUP):
        columns, places = [], []
        for owner in range(group * GROUP, (group + 1) * GROUP):
            got = got_ref[owner]
            high = got.astype(BF16).astype(F32)
            low = got - high
            mine = row == wide(got[6:7])
            zero = jnp.zeros((), BF16)
            parts = [jnp.where(mine, wide(part[r : r + 1]), zero) for part in (high, low) for r in range(PARTS)]
            columns.append(jnp.concatenate(parts, axis=0))
            places.append(got[7:8])
        spread = jnp.concatenate(columns, axis=1)
        added = lax.dot_general(spread, cells_of(places), NT, preferred_element_type=F32)
        side = group % 2
        grids[side] = added if grids[side] is None else grids[side] + added
    grid = grids[0] + jnp.where(got_ref[0, 7:8, :1] > -2.0, grids[1], 0.0)
    grid = (grid[: PARTS * ROWS] + grid[PARTS * ROWS :]).reshape(PLANES, 2, ROWS, CELLS)
    pieces = [
        jnp.concatenate([grid[:, part, :, c * HALF : (c + 1) * HALF] for part in range(2)], axis=2)
        for c in range(CHUNK)
    ]
    lined = jnp.stack(pieces, axis=1).reshape(PLANES * HALF, LANES)
    high, low = split(lined)
    middle = dot(jnp.concatenate([high, low], axis=1), second_pair[...]) + dot(high, second_low[...])
    returned = []
    for plane in range(PLANES):
        high, low = split(middle[plane * HALF : (plane + 1) * HALF])
        both = dot(first_all[...], jnp.concatenate([high, high, low], axis=0))
        real_part = both[:NG, :LANES] - both[NG:, LANES:]
        imag_part = both[NG:, :LANES] + both[:NG, LANES:]
        if stage == "first":
            outs[1][plane] = real_part * real_part + imag_part * imag_part
        if stage == "last":
            outs[1][...] = real_part * real_part + imag_part * imag_part - other_ref[plane]
            pack_cells(outs[1], outs[0], plane * FLAT)
            continue
        weight = weight_ref[plane * NG : (plane + 1) * NG]
        field = jnp.concatenate([real_part * weight, imag_part * weight], axis=1)
        high, low = split(field)
        both = dot(back_all[...], jnp.concatenate([high, high, low], axis=0))
        returned.append(
            jnp.concatenate(
                [both[:HALF, :LANES] + both[HALF:, LANES:], both[:HALF, LANES:] - both[HALF:, :LANES]],
                axis=1,
            )
        )
    if stage == "last":
        return
    high, low = split(jnp.concatenate(returned, axis=0))
    rows = dot(high, inner_high[...]) + dot(low, inner_high[...]) + dot(high, inner_low[...])
    rows = rows.reshape(PLANES, CHUNK, ROWS, LANES)
    pieces = [
        jnp.concatenate([rows[:, c, :, part * HALF : (part + 1) * HALF] for c in range(CHUNK)], axis=2)
        for part in range(2)
    ]
    high, low = split(jnp.stack(pieces, axis=1).reshape(PARTS * ROWS, CELLS))
    both = jnp.concatenate([high, low], axis=0)
    tail = jnp.zeros((2, SLOTS), F32)

    row = lax.broadcasted_iota(jnp.int32, (ROWS, SLOTS), 0).astype(F32)
    for owner in range(0, OWNERS, 2):
        pair = (owner, owner + 1)
        found = dot(both, cells_of([got_ref[o][7:8] for o in pair]))
        found = (found[: PARTS * ROWS] + found[PARTS * ROWS :]).reshape(PARTS, ROWS, 2 * SLOTS)
        for side, o in enumerate(pair):
            mine = row == got_ref[o][6:7]
            chosen = jnp.where(mine[None], found[:, :, side * SLOTS : (side + 1) * SLOTS], 0.0)
            outs[0][o] = jnp.concatenate([jnp.sum(chosen, axis=1), tail], axis=0)


def call(kernel, name, shapes, **more):
    return pl.pallas_call(
        kernel,
        **more,
        out_shape=tuple(jax.ShapeDtypeStruct(s, F32) for s in shapes),
        name=name,
        compiler_params=pltpu.CompilerParams(vmem_limit_bytes=32 << 20),
    )


def plane_call(stage, got, other, plane_tables):
    wire = (OWNERS, 8, SLOTS)
    cells = (PLANES, NG, LANES)
    shapes = {"first": (wire, cells, (PLANES * NG, LANES), (PLANES * FLAT, LANES)), "next": (wire,), "last": ((PLANES * FLAT, LANES),)}[stage]
    more = {"scratch_shapes": [pltpu.VMEM((NG, LANES), F32)]} if stage == "last" else {}
    return call(functools.partial(plane_kernel, stage), "plane_" + stage, shapes, **more)(got, other, *plane_tables)


def exchange(rows):
    return lax.all_to_all(rows, ("x", "z"), split_axis=0, concat_axis=0, tiled=True)


def swap(values, axis, mask):
    size = lax.axis_size(axis)
    return lax.ppermute(values, axis, [(s, s ^ mask) for s in range(size)])


def shards(psi, potential, stick_column, stick_length):
    stick_np, plane_np = tables()
    stick_table = jnp.asarray(stick_np)
    plane_tables = tuple(map(jnp.asarray, plane_np))
    wire, state = (OWNERS, 8, SLOTS), (SLOTS, LANES)
    kept = (
        pltpu.VMEM((2, SLOTS, LANES), F32),
        pltpu.VMEM((SLOTS,), jnp.int32),
        pltpu.VMEM((SLOTS,), jnp.int32),
        pltpu.VMEM(stick_np.shape, BF16),
        pltpu.SemaphoreType.DMA((5,)),
    )
    begin = call(
        start_kernel,
        "start",
        (state, state, (8, SLOTS), wire, potential.shape),
        in_specs=[pl.BlockSpec(memory_space=pltpu.HBM)] * 5,
        scratch_shapes=kept,
    )
    term, kinetic, places, rows, kept_potential = begin(
        *(
            pltpu.with_memory_space_constraint(source, pltpu.HBM)
            for source in (psi.reshape(2, SLOTS, LANES), stick_column, stick_length, stick_table, potential)
        )
    )
    total = term
    before = weight = flat = None
    for power in range(1, 4):
        got = exchange(rows)
        if power == 1:
            rows, before, weight, flat = plane_call("first", got, kept_potential, plane_tables)
        else:
            (rows,) = plane_call("next", got, weight, plane_tables)
        got = exchange(rows)
        last = power == 3
        shapes = (state, wire) if last else (state, state, wire)
        given = call(functools.partial(stick_kernel, power, last), f"stick_{power}", shapes)(
            got, term, total, kinetic, places, stick_table
        )
        if last:
            total, rows = given
        else:
            total, term, rows = given
    (change,) = plane_call("last", exchange(rows), before, plane_tables)
    near, far, across = (swap(change, "y", mask) for mask in (1, 2, 3))
    (psi_new,) = call(finish_kernel, "finish", ((2, SLOTS, LANES),))(total, places)
    change = (change + near) + (far + across)
    change = change + swap(change, "core", 1)
    added = flat + LINEAR_GAIN * change + CUBIC_GAIN * change * change * change
    return psi_new.reshape(2, 1, SLOTS, LANES), added.reshape(PLANES, NG * NG)


def solution(mesh):
    fine = Mesh(mesh.devices.reshape(4, 2, 4, 8), ("y", "core", "x", "z"))
    band, plane = ("y", "core"), ("x", "z")
    in_specs = (P(None, band, plane, None), P(plane, None), P(plane), P(plane))
    out_specs = (P(None, band, plane, None), P(plane, None))
    return jax.shard_map(shards, mesh=fine, in_specs=in_specs, out_specs=out_specs, check_vma=False)
```
